128 devices in a mesh: ia: 8 (over z, y_hi), ja: 8 (over x, core), aux: 2 (over y_lo).
Axes of the slice: x: 4, y: 4 (y_hi: 2, y_lo: 2; y = y_hi * 2 + y_lo), z: 4, core: 2. Of those that a mesh axis runs over, the one named last changes fastest.
Arguments:
- raw_integrals: bfloat16 [2048, 24, 512], P(('ia', 'ja', 'aux')), may hold values from -0.5 to 0.5
- metric_root: bfloat16 [2048, 2048], replicated, may hold values from -0.125 to 0.125
- eps_occ: float32 [24], replicated, may hold values from -2 to -0.3
- eps_vir: float32 [512], replicated, may hold values from 0.3 to 3
Outputs:
- gamma: float32 [2048, 24, 512], P('ja', 'ia', 'aux')
The draws below stay inside these ranges and needn't reach their ends.
All inputs are finite; a program needn't handle non-finite values.
Results may differ from the reference program's by a relative error of at most 0.0022.
Values may be sent and summed in bfloat16 or wider, within the bound.
A program may use at most 128 MiB of HBM per device.

```python
import math
import jax
import jax.numpy as jnp
from jax import lax

V = 512
NAUX = 2048
OCC = 24


def block_levels(own_key, shape, cuts, smallest, high):
    def one(dim, shards_of):
        heights = jax.random.uniform(jax.random.fold_in(jax.random.fold_in(own_key, 6), dim), (shards_of,), jnp.float32, smallest / len(cuts), high / len(cuts))
        return jnp.repeat(jnp.exp(heights), shape[dim] // shards_of).reshape((-1,) + (1,) * (len(shape) - dim - 1))

    gain = one(*cuts[0])
    for cut in cuts[1:]:
        gain = gain * one(*cut)
    return gain


def gaussian(rng, extent, scale, limit, cuts=(), held_as=jnp.bfloat16):
    result = jax.random.normal(rng, extent, jnp.float32) * scale
    if len(cuts) > 0:
        result = block_levels(rng, extent, cuts, -0.22, 0.18) * result
    return jnp.clip(result, min=-limit, max=limit).astype(held_as)


def setup_inputs(seed: int = 0) -> dict:
    key_of = jax.random.split(jax.random.key(seed), 5)
    raw_integrals = gaussian(key_of[0], (NAUX, OCC, V), 0.07, 0.5, ((0, 128),))
    metric_root = gaussian(key_of[1], (NAUX, NAUX), NAUX ** -0.5, 0.125)
    eps_occ = jnp.clip(jax.random.uniform(key_of[2], (OCC,), jnp.float32, -2.0, -0.3), -2.0, -0.3)
    eps_vir = jnp.clip(jnp.exp(jax.random.uniform(key_of[3], (V,), jnp.float32, math.log(0.3), math.log(3.0))), 0.3, 3.0)
    return {"raw_integrals": raw_integrals, "metric_root": metric_root, "eps_occ": eps_occ, "eps_vir": eps_vir}


def reference(raw_integrals, metric_root, eps_occ, eps_vir):
    fitted = lax.dot_general(metric_root, raw_integrals.reshape(NAUX, OCC * V), (((0,), (0,)), ((), ())), preferred_element_type=jnp.float32).astype(jnp.bfloat16)
    fitted_flat = fitted.astype(jnp.float32)

    def per_occupied(index):
        column = lax.dynamic_slice_in_dim(fitted_flat, (index * V).astype(jnp.int32), V, 1)
        coulomb = jnp.dot(column.T, fitted_flat, preferred_element_type=jnp.float32).reshape(V, OCC, V)
        energy_i = lax.dynamic_index_in_dim(eps_occ, index, 0, keepdims=False)
        denominator = eps_vir[:, None, None] + eps_vir[None, None, :] - energy_i - eps_occ[None, :, None]
        amplitude = ((2.0 * coulomb - coulomb.transpose(2, 1, 0)) / denominator).astype(jnp.bfloat16)
        amplitude = lax.optimization_barrier(amplitude).astype(jnp.float32)
        return jnp.dot(fitted_flat, amplitude.reshape(V, OCC * V).T, preferred_element_type=jnp.float32)

    gamma = lax.map(per_occupied, jnp.arange(OCC, dtype=jnp.int32))
    return gamma.transpose(1, 0, 2)
```

```python
import functools

import jax
import jax.numpy as jnp
from jax import lax
from jax.experimental import pallas as pl
from jax.experimental.pallas import tpu as pltpu
from jax.sharding import PartitionSpec as P

OB = 3
V = 512
NC = 4
QC = 512
LA = 256
HALF = 256
ROWS = OB * HALF
F32 = jnp.float32
BF16 = jnp.bfloat16
MESH = pl.DeviceIdType.MESH


def kernel(
    got_ref, met_hbm, eocc_ref, evr_ref, evc_ref, out_ref,
    fi, fj, met, acc, amp, gown, sib_s, sib_r, opp_s, opp_r, rs_s, rs_r,
    met_sem, ss, rs, gs, gr,
):
    ia = lax.axis_index("ia")
    ja = lax.axis_index("ja")
    aux = lax.axis_index("aux")
    z, yh = lax.div(ia, 2), lax.rem(ia, 2)
    x, core = lax.div(ja, 2), lax.rem(ja, 2)
    y = yh * 2 + aux

    def step(v, d):
        return lax.rem(v + (d + 4), 4)

    def ydev(d):
        w = step(y, d)
        return {"ia": z * 2 + lax.div(w, 2), "ja": ja, "aux": lax.rem(w, 2)}

    def zdev(d):
        return {"ia": step(z, d) * 2 + yh, "ja": ja, "aux": aux}

    def xdev(d):
        return {"ia": ia, "ja": step(x, d) * 2 + core, "aux": aux}

    sib = {"ia": ia, "ja": x * 2 + (1 - core), "aux": aux}
    ypart = {"ia": ia, "ja": ja, "aux": 1 - aux}

    met_copies = [
        pltpu.make_async_copy(met_hbm.at[:, pl.ds(c * QC, QC)], met.at[c], met_sem.at[c])
        for c in range(NC)
    ]
    for c in range(NC):
        met_copies[c].start()

    barrier = pltpu.get_barrier_semaphore()
    for dev in (ydev(1), ydev(-1), zdev(1), zdev(-1), xdev(1), xdev(-1), sib):
        pl.semaphore_signal(barrier, inc=1, device_id=dev, device_id_type=MESH)
    pl.semaphore_wait(barrier, 7)

    pending = []

    def put(ref, c, n, dev):
        copy = pltpu.make_async_remote_copy(
            src_ref=ref, dst_ref=ref, send_sem=ss.at[c, n], recv_sem=rs.at[c, n],
            device_id=dev, device_id_type=MESH,
        )
        copy.start()
        pending.append(copy)

    def arrived(ref, c, n):
        pltpu.make_async_remote_copy(
            src_ref=ref, dst_ref=ref, send_sem=ss.at[c, n], recv_sem=rs.at[c, n],
            device_id=sib, device_id_type=MESH,
        ).wait_recv()

    def fja(c, zz, yy, r=slice(None)):
        return fj.at[c, :, zz, yy, r, pl.ds(0, LA)]

    def fjb(c, zz, yy, r=slice(None)):
        return fj.at[c, :, zz, yy, r, pl.ds(LA, QC - LA)]

    lo, hi = pl.ds(0, 16), pl.ds(16, 16)
    first2, last2 = pl.ds(0, 2), pl.ds(2, 2)
    every = slice(None)
    yp, ym, y2 = step(y, 1), step(y, -1), step(y, 2)
    zp, zm, z2 = step(z, 1), step(z, -1), step(z, 2)
    xp, xm, x2 = step(x, 1), step(x, -1), step(x, 2)

    def fit(c):
        met_copies[c].wait()
        r = lax.dot_general(
            got_ref[...], met[c], (((0,), (0,)), ((), ())), preferred_element_type=F32
        ).astype(BF16)
        for k in range(OB):
            fi[c, k, x, core, aux] = r[32 * k : 32 * k + 32]
            fj[c, k, z, y] = r[128 + 32 * k : 160 + 32 * k]

    def p0(c):
        put(fja(c, z, y), c, 0, ydev(1))
        put(fja(c, z, y), c, 1, ydev(-1))
        put(fjb(c, z, y), c, 2, zdev(1))
        put(fjb(c, z, y), c, 3, zdev(-1))
        put(fi.at[c, :, x, core, aux], c, 4, ypart)

    def p1(c):
        arrived(fi.at[c, :, x, core, 1 - aux], c, 4)
        put(fi.at[c, :, x, core], c, 9, xdev(1))
        put(fi.at[c, :, x, core], c, 10, xdev(-1))
        put(fi.at[c, :, x, core], c, 11, sib)
        arrived(fja(c, z, ym), c, 0)
        put(fja(c, z, ym, lo), c, 5, ydev(1))
        arrived(fja(c, z, yp), c, 1)
        put(fja(c, z, yp, hi), c, 6, ydev(-1))
        arrived(fjb(c, zm, y), c, 2)
        put(fjb(c, zm, y, lo), c, 7, zdev(1))
        arrived(fjb(c, zp, y), c, 3)
        put(fjb(c, zp, y, hi), c, 8, zdev(-1))

    def p2(c):
        arrived(fja(c, z, y2, lo), c, 5)
        arrived(fja(c, z, y2, hi), c, 6)
        put(fja(c, z, every), c, 12, zdev(1))
        put(fja(c, z, every), c, 13, zdev(-1))
        arrived(fjb(c, z2, y, lo), c, 7)
        arrived(fjb(c, z2, y, hi), c, 8)
        put(fjb(c, every, y), c, 14, ydev(1))
        put(fjb(c, every, y), c, 15, ydev(-1))
        arrived(fi.at[c, :, xm, core], c, 9)
        put(fi.at[c, :, xm, core, 0], c, 16, xdev(1))
        put(fi.at[c, :, xm, core], c, 17, sib)
        arrived(fi.at[c, :, xp, core], c, 10)
        put(fi.at[c, :, xp, core, 1], c, 18, xdev(-1))
        put(fi.at[c, :, xp, core], c, 19, sib)

    def p3(c):
        arrived(fja(c, zm, every), c, 12)
        put(fja(c, zm, first2), c, 20, zdev(1))
        arrived(fja(c, zp, every), c, 13)
        put(fja(c, zp, last2), c, 21, zdev(-1))
        arrived(fjb(c, every, ym), c, 14)
        put(fjb(c, first2, ym), c, 22, ydev(1))
        arrived(fjb(c, every, yp), c, 15)
        put(fjb(c, last2, yp), c, 23, ydev(-1))
        arrived(fi.at[c, :, x2, core, 0], c, 16)
        arrived(fi.at[c, :, x2, core, 1], c, 18)
        put(fi.at[c, :, x2, core], c, 24, sib)

    def p4(c):
        arrived(fja(c, z2, first2), c, 20)
        arrived(fja(c, z2, last2), c, 21)
        arrived(fjb(c, first2, y2), c, 22)
        arrived(fjb(c, last2, y2), c, 23)
        other = 1 - core
        arrived(fi.at[c, :, x, other], c, 11)
        arrived(fi.at[c, :, xm, other], c, 17)
        arrived(fi.at[c, :, xp, other], c, 19)
        arrived(fi.at[c, :, x2, other], c, 24)

    over_q = (((1,), (1,)), ((), ()))

    def coulomb(c):
        def direct(l, carry):
            part = lax.dot_general(
                fi[c, :, pl.ds(2 * aux, 2)].reshape(ROWS, QC),
                fj[c, l].reshape(V, QC),
                over_q,
                preferred_element_type=F32,
            )
            for k in range(OB):
                term = 2.0 * part[k * HALF : (k + 1) * HALF]
                acc[k, l] = term if c == 0 else acc[k, l] + term
            return carry

        def swap(k, carry):
            part = lax.dot_general(
                fj[c, :, pl.ds(2 * aux, 2)].reshape(ROWS, QC),
                fi[c, k].reshape(V, QC),
                over_q,
                preferred_element_type=F32,
            )
            for l in range(OB):
                acc[k, l] = acc[k, l] - part[l * HALF : (l + 1) * HALF]
            return carry

        lax.fori_loop(0, OB, direct, 0)
        lax.fori_loop(0, OB, swap, 0)

    fit(0)
    p0(0)
    fit(1)
    p0(1)
    p1(0)
    fit(2)
    p0(2)
    p1(1)
    p2(0)
    fit(3)
    p0(3)
    p1(2)
    p2(1)
    p1(3)
    p3(0)
    p2(2)
    p4(0)
    coulomb(0)
    p3(1)
    p2(3)
    p4(1)
    coulomb(1)
    p3(2)
    p4(2)
    p3(3)
    coulomb(2)
    p4(3)
    coulomb(3)

    for k in range(OB):
        for l in range(OB):
            den = evc_ref[...] + evr_ref[...] - eocc_ref[OB * ia + k] - eocc_ref[OB * ja + l]
            amp[k, :, l * V : (l + 1) * V] = (acc[k, l] / den).astype(BF16)

    def partial(block, half):
        lanes = pl.ds(pl.multiple_of(half * HALF, HALF), HALF)
        total = None
        for l in range(OB):
            term = jnp.dot(
                amp[:, :, l * V : (l + 1) * V].reshape(ROWS, V),
                fj[block, l, :, :, :, lanes].reshape(V, HALF),
                preferred_element_type=F32,
            )
            total = term if total is None else total + term
        return total

    def send(src, dst, n, dev):
        copy = pltpu.make_async_remote_copy(
            src_ref=src, dst_ref=dst, send_sem=gs.at[n], recv_sem=gr.at[n],
            device_id=dev, device_id_type=MESH,
        )
        copy.start()
        pending.append(copy)

    def landed(dst, n):
        pltpu.make_async_remote_copy(
            src_ref=dst, dst_ref=dst, send_sem=gs.at[n], recv_sem=gr.at[n],
            device_id=sib, device_id_type=MESH,
        ).wait_recv()

    H = ROWS // 2
    top, bottom = pl.ds(0, H), pl.ds(H, H)

    def both_cores(m, block):
        sib_s[m] = partial(block, 1 - core).astype(BF16)
        send(sib_s.at[m], sib_r.at[m], m, sib)
        gown[m] = partial(block, core)

    both_cores(0, x2)
    both_cores(1, xp)
    landed(sib_r.at[0], 0)
    opp_s[...] = (gown[0] + sib_r[0].astype(F32)).astype(BF16)
    send(opp_s.at[top], opp_r.at[top], 4, xdev(1))
    send(opp_s.at[bottom], opp_r.at[bottom], 5, xdev(-1))
    both_cores(2, xm)
    landed(sib_r.at[1], 1)
    rs_s[0, bottom] = (gown[1, bottom] + sib_r[1, bottom].astype(F32)).astype(BF16)
    send(rs_s.at[0, bottom], rs_r.at[0, bottom], 6, xdev(1))
    both_cores(3, x)
    landed(sib_r.at[2], 2)
    rs_s[1, top] = (gown[2, top] + sib_r[2, top].astype(F32)).astype(BF16)
    send(rs_s.at[1, top], rs_r.at[1, top], 7, xdev(-1))
    landed(opp_r.at[top], 4)
    rs_s[0, top] = (
        gown[1, top] + sib_r[1, top].astype(F32) + opp_r[top].astype(F32)
    ).astype(BF16)
    send(rs_s.at[0, top], rs_r.at[0, top], 8, xdev(1))
    landed(opp_r.at[bottom], 5)
    rs_s[1, bottom] = (
        gown[2, bottom] + sib_r[2, bottom].astype(F32) + opp_r[bottom].astype(F32)
    ).astype(BF16)
    send(rs_s.at[1, bottom], rs_r.at[1, bottom], 9, xdev(-1))
    landed(sib_r.at[3], 3)
    landed(rs_r.at[0, bottom], 6)
    landed(rs_r.at[1, top], 7)
    landed(rs_r.at[0, top], 8)
    landed(rs_r.at[1, bottom], 9)
    for k in range(OB):
        r = slice(k * HALF, (k + 1) * HALF)
        total = (
            gown[3, r]
            + sib_r[3, r].astype(F32)
            + rs_r[0, r].astype(F32)
            + rs_r[1, r].astype(F32)
        )
        out_ref[k] = total.T
    for copy in pending:
        copy.wait_send()


def body(raw_integrals, metric_root, eps_occ, eps_vir):
    aux_index = lax.axis_index("aux")
    pieces = raw_integrals.shape[0]
    aux_total = metric_root.shape[0]
    narrow = V // 16
    by_slice = raw_integrals.reshape(pieces, 8, OB, 16, narrow)
    blocks = by_slice.transpose(1, 3, 0, 2, 4).reshape(8, 8, 2, pieces, OB * narrow)
    blocks = jnp.pad(blocks, ((0, 0),) * 4 + ((0, 128 - OB * narrow),))
    both = jnp.concatenate([blocks, blocks.transpose(1, 0, 2, 3, 4)], axis=4).reshape(128, pieces, 256)
    got = lax.all_to_all(both, ("ia", "ja", "aux"), split_axis=0, concat_axis=0, tiled=True)
    got = got.reshape(aux_total, 256)
    ev_half = lax.dynamic_slice_in_dim(eps_vir, aux_index * HALF, HALF, 0)
    vmem = pl.BlockSpec(memory_space=pltpu.VMEM)
    out = pl.pallas_call(
        kernel,
        out_shape=jax.ShapeDtypeStruct((OB, HALF, HALF), F32),
        in_specs=[
            vmem,
            pl.BlockSpec(memory_space=pl.ANY),
            pl.BlockSpec(memory_space=pltpu.SMEM),
            vmem,
            vmem,
        ],
        out_specs=vmem,
        scratch_shapes=[
            pltpu.VMEM((NC, OB, 4, 2, 2, 32, QC), BF16),
            pltpu.VMEM((NC, OB, 4, 4, 32, QC), BF16),
            pltpu.VMEM((NC, aux_total, QC), BF16),
            pltpu.VMEM((OB, OB, HALF, V), F32),
            pltpu.VMEM((OB, HALF, OB * V), BF16),
            pltpu.VMEM((4, ROWS, HALF), F32),
            pltpu.VMEM((4, ROWS, HALF), BF16),
            pltpu.VMEM((4, ROWS, HALF), BF16),
            pltpu.VMEM((ROWS, HALF), BF16),
            pltpu.VMEM((ROWS, HALF), BF16),
            pltpu.VMEM((2, ROWS, HALF), BF16),
            pltpu.VMEM((2, ROWS, HALF), BF16),
            pltpu.SemaphoreType.DMA((NC,)),
            pltpu.SemaphoreType.DMA((NC, 25)),
            pltpu.SemaphoreType.DMA((NC, 25)),
            pltpu.SemaphoreType.DMA((10,)),
            pltpu.SemaphoreType.DMA((10,)),
        ],
        compiler_params=pltpu.CompilerParams(
            collective_id=0, has_side_effects=True, vmem_limit_bytes=60 * 2**20
        ),
    )(got, metric_root, eps_occ, eps_vir.reshape(1, V), ev_half.reshape(HALF, 1))
    return out.transpose(1, 0, 2)


def solution(mesh):
    in_specs = (P(("ia", "ja", "aux"), None, None), P(), P(), P())
    out_specs = P("ja", "ia", "aux")
    return jax.shard_map(body, mesh=mesh, in_specs=in_specs, out_specs=out_specs, check_vma=False)
```

```python
import functools

import jax
import jax.numpy as jnp
from jax import lax
from jax.experimental import pallas as pl
from jax.experimental.pallas import tpu as pltpu
from jax.sharding import PartitionSpec as P

OB = 3
V = 512
NC = 4
QC = 512
LA = 256
HALF = 256
ROWS = OB * HALF
F32 = jnp.float32
BF16 = jnp.bfloat16
MESH = pl.DeviceIdType.MESH


def kernel(
    got_ref, met_hbm, eocc_ref, evr_ref, evc_ref, out_ref,
    fi, fj, met, acc, amp, gown, sib_s, sib_r, opp_s, opp_r, rs_s, rs_r,
    met_sem, ss, rs, gs, gr,
):
    ia = lax.axis_index("ia")
    ja = lax.axis_index("ja")
    aux = lax.axis_index("aux")
    z, yh = lax.div(ia, 2), lax.rem(ia, 2)
    x, core = lax.div(ja, 2), lax.rem(ja, 2)
    y = yh * 2 + aux

    def step(v, d):
        return lax.rem(v + (d + 4), 4)

    def ydev(d):
        w = step(y, d)
        return {"ia": z * 2 + lax.div(w, 2), "ja": ja, "aux": lax.rem(w, 2)}

    def zdev(d):
        return {"ia": step(z, d) * 2 + yh, "ja": ja, "aux": aux}

    def xdev(d):
        return {"ia": ia, "ja": step(x, d) * 2 + core, "aux": aux}

    sib = {"ia": ia, "ja": x * 2 + (1 - core), "aux": aux}
    ypart = {"ia": ia, "ja": ja, "aux": 1 - aux}

    met_copies = [
        pltpu.make_async_copy(met_hbm.at[:, pl.ds(c * QC, QC)], met.at[c], met_sem.at[c])
        for c in range(NC)
    ]
    for c in range(NC):
        met_copies[c].start()

    barrier = pltpu.get_barrier_semaphore()
    for dev in (ydev(1), ydev(-1), zdev(1), zdev(-1), xdev(1), xdev(-1), sib):
        pl.semaphore_signal(barrier, inc=1, device_id=dev, device_id_type=MESH)
    pl.semaphore_wait(barrier, 7)

    pending = []

    def put(ref, c, n, dev):
        copy = pltpu.make_async_remote_copy(
            src_ref=ref, dst_ref=ref, send_sem=ss.at[c, n], recv_sem=rs.at[c, n],
            device_id=dev, device_id_type=MESH,
        )
        copy.start()
        pending.append(copy)

    def arrived(ref, c, n):
        pltpu.make_async_remote_copy(
            src_ref=ref, dst_ref=ref, send_sem=ss.at[c, n], recv_sem=rs.at[c, n],
            device_id=sib, device_id_type=MESH,
        ).wait_recv()

    def fja(c, zz, yy, r=slice(None)):
        return fj.at[c, :, zz, yy, r, pl.ds(0, LA)]

    def fjb(c, zz, yy, r=slice(None)):
        return fj.at[c, :, zz, yy, r, pl.ds(LA, QC - LA)]

    lo, hi = pl.ds(0, 16), pl.ds(16, 16)
    first2, last2 = pl.ds(0, 2), pl.ds(2, 2)
    every = slice(None)
    yp, ym, y2 = step(y, 1), step(y, -1), step(y, 2)
    zp, zm, z2 = step(z, 1), step(z, -1), step(z, 2)
    xp, xm, x2 = step(x, 1), step(x, -1), step(x, 2)

    def fit(c):
        met_copies[c].wait()
        r = lax.dot_general(
            got_ref[...], met[c], (((0,), (0,)), ((), ())), preferred_element_type=F32
        ).astype(BF16)
        for k in range(OB):
            fi[c, k, x, core, aux] = r[32 * k : 32 * k + 32]
            fj[c, k, z, y] = r[128 + 32 * k : 160 + 32 * k]

    def p0(c):
        put(fja(c, z, y), c, 0, ydev(1))
        put(fja(c, z, y), c, 1, ydev(-1))
        put(fjb(c, z, y), c, 2, zdev(1))
        put(fjb(c, z, y), c, 3, zdev(-1))
        put(fi.at[c, :, x, core, aux], c, 4, ypart)

    def p1(c):
        arrived(fi.at[c, :, x, core, 1 - aux], c, 4)
        put(fi.at[c, :, x, core], c, 9, xdev(1))
        put(fi.at[c, :, x, core], c, 10, xdev(-1))
        put(fi.at[c, :, x, core], c, 11, sib)
        arrived(fja(c, z, ym), c, 0)
        put(fja(c, z, ym, lo), c, 5, ydev(1))
        arrived(fja(c, z, yp), c, 1)
        put(fja(c, z, yp, hi), c, 6, ydev(-1))
        arrived(fjb(c, zm, y), c, 2)
        put(fjb(c, zm, y, lo), c, 7, zdev(1))
        arrived(fjb(c, zp, y), c, 3)
        put(fjb(c, zp, y, hi), c, 8, zdev(-1))

    def p2(c):
        arrived(fja(c, z, y2, lo), c, 5)
        arrived(fja(c, z, y2, hi), c, 6)
        put(fja(c, z, every), c, 12, zdev(1))
        put(fja(c, z, every), c, 13, zdev(-1))
        arrived(fjb(c, z2, y, lo), c, 7)
        arrived(fjb(c, z2, y, hi), c, 8)
        put(fjb(c, every, y), c, 14, ydev(1))
        put(fjb(c, every, y), c, 15, ydev(-1))
        arrived(fi.at[c, :, xm, core], c, 9)
        put(fi.at[c, :, xm, core, 0], c, 16, xdev(1))
        put(fi.at[c, :, xm, core], c, 17, sib)
        arrived(fi.at[c, :, xp, core], c, 10)
        put(fi.at[c, :, xp, core, 1], c, 18, xdev(-1))
        put(fi.at[c, :, xp, core], c, 19, sib)

    def p3(c):
        arrived(fja(c, zm, every), c, 12)
        put(fja(c, zm, first2), c, 20, zdev(1))
        arrived(fja(c, zp, every), c, 13)
        put(fja(c, zp, last2), c, 21, zdev(-1))
        arrived(fjb(c, every, ym), c, 14)
        put(fjb(c, first2, ym), c, 22, ydev(1))
        arrived(fjb(c, every, yp), c, 15)
        put(fjb(c, last2, yp), c, 23, ydev(-1))
        arrived(fi.at[c, :, x2, core, 0], c, 16)
        arrived(fi.at[c, :, x2, core, 1], c, 18)
        put(fi.at[c, :, x2, core], c, 24, sib)

    def p4(c):
        arrived(fja(c, z2, first2), c, 20)
        arrived(fja(c, z2, last2), c, 21)
        arrived(fjb(c, first2, y2), c, 22)
        arrived(fjb(c, last2, y2), c, 23)
        other = 1 - core
        arrived(fi.at[c, :, x, other], c, 11)
        arrived(fi.at[c, :, xm, other], c, 17)
        arrived(fi.at[c, :, xp, other], c, 19)
        arrived(fi.at[c, :, x2, other], c, 24)

    over_q = (((1,), (1,)), ((), ()))

    def coulomb(c):
        def direct(l, carry):
            part = lax.dot_general(
                fi[c, :, pl.ds(2 * aux, 2)].reshape(ROWS, QC),
                fj[c, l].reshape(V, QC),
                over_q,
                preferred_element_type=F32,
            )
            for k in range(OB):
                term = 2.0 * part[k * HALF : (k + 1) * HALF]
                acc[k, l] = term if c == 0 else acc[k, l] + term
            return carry

        def swap(k, carry):
            part = lax.dot_general(
                fj[c, :, pl.ds(2 * aux, 2)].reshape(ROWS, QC),
                fi[c, k].reshape(V, QC),
                over_q,
                preferred_element_type=F32,
            )
            for l in range(OB):
                acc[k, l] = acc[k, l] - part[l * HALF : (l + 1) * HALF]
            return carry

        lax.fori_loop(0, OB, direct, 0)
        lax.fori_loop(0, OB, swap, 0)

    fit(0)
    p0(0)
    fit(1)
    p0(1)
    p1(0)
    fit(2)
    p0(2)
    p1(1)
    p2(0)
    fit(3)
    p0(3)
    p1(2)
    p2(1)
    p1(3)
    p3(0)
    p2(2)
    p4(0)
    coulomb(0)
    p3(1)
    p2(3)
    p4(1)
    coulomb(1)
    p3(2)
    p4(2)
    p3(3)
    coulomb(2)
    p4(3)
    coulomb(3)

    for k in range(OB):
        for l in range(OB):
            den = evc_ref[...] + evr_ref[...] - eocc_ref[OB * ia + k] - eocc_ref[OB * ja + l]
            amp[k, :, l * V : (l + 1) * V] = (acc[k, l] / den).astype(BF16)

    def partial(block, half):
        lanes = pl.ds(pl.multiple_of(half * HALF, HALF), HALF)
        total = None
        for l in range(OB):
            term = jnp.dot(
                amp[:, :, l * V : (l + 1) * V].reshape(ROWS, V),
                fj[block, l, :, :, :, lanes].reshape(V, HALF),
                preferred_element_type=F32,
            )
            total = term if total is None else total + term
        return total

    def send(src, dst, n, dev):
        copy = pltpu.make_async_remote_copy(
            src_ref=src, dst_ref=dst, send_sem=gs.at[n], recv_sem=gr.at[n],
            device_id=dev, device_id_type=MESH,
        )
        copy.start()
        pending.append(copy)

    def landed(dst, n):
        pltpu.make_async_remote_copy(
            src_ref=dst, dst_ref=dst, send_sem=gs.at[n], recv_sem=gr.at[n],
            device_id=sib, device_id_type=MESH,
        ).wait_recv()

    H = ROWS // 2
    top, bottom = pl.ds(0, H), pl.ds(H, H)

    def both_cores(m, block):
        sib_s[m] = partial(block, 1 - core).astype(BF16)
        send(sib_s.at[m], sib_r.at[m], m, sib)
        gown[m] = partial(block, core)

    both_cores(0, x2)
    both_cores(1, xp)
    landed(sib_r.at[0], 0)
    opp_s[...] = (gown[0] + sib_r[0].astype(F32)).astype(BF16)
    send(opp_s.at[top], opp_r.at[top], 4, xdev(1))
    send(opp_s.at[bottom], opp_r.at[bottom], 5, xdev(-1))
    both_cores(2, xm)
    landed(sib_r.at[1], 1)
    rs_s[0, bottom] = (gown[1, bottom] + sib_r[1, bottom].astype(F32)).astype(BF16)
    send(rs_s.at[0, bottom], rs_r.at[0, bottom], 6, xdev(1))
    both_cores(3, x)
    landed(sib_r.at[2], 2)
    rs_s[1, top] = (gown[2, top] + sib_r[2, top].astype(F32)).astype(BF16)
    send(rs_s.at[1, top], rs_r.at[1, top], 7, xdev(-1))
    landed(opp_r.at[top], 4)
    rs_s[0, top] = (
        gown[1, top] + sib_r[1, top].astype(F32) + opp_r[top].astype(F32)
    ).astype(BF16)
    send(rs_s.at[0, top], rs_r.at[0, top], 8, xdev(1))
    landed(opp_r.at[bottom], 5)
    rs_s[1, bottom] = (
        gown[2, bottom] + sib_r[2, bottom].astype(F32) + opp_r[bottom].astype(F32)
    ).astype(BF16)
    send(rs_s.at[1, bottom], rs_r.at[1, bottom], 9, xdev(-1))
    landed(sib_r.at[3], 3)
    landed(rs_r.at[0, bottom], 6)
    landed(rs_r.at[1, top], 7)
    landed(rs_r.at[0, top], 8)
    landed(rs_r.at[1, bottom], 9)
    for k in range(OB):
        r = slice(k * HALF, (k + 1) * HALF)
        total = (
            gown[3, r]
            + sib_r[3, r].astype(F32)
            + rs_r[0, r].astype(F32)
            + rs_r[1, r].astype(F32)
        )
        out_ref[k] = total.T
    for copy in pending:
        copy.wait_send()


def spread_kernel(raw_ref, got_ref, send, own_sem, send_sem, recv_sem):
    ia = lax.axis_index("ia")
    ja = lax.axis_index("ja")
    aux = lax.axis_index("aux")
    me = ia * 16 + ja * 2 + aux
    pieces = raw_ref.shape[0]
    occ = raw_ref.shape[1]
    n = pieces * occ
    row = lax.broadcasted_iota(jnp.int32, (n, n), 0)
    col = lax.broadcasted_iota(jnp.int32, (n, n), 1)
    pick = ((row & 15) * occ + (row >> 4) == col).astype(F32).astype(BF16)
    by_occ = jnp.dot(pick, raw_ref[...].reshape(n, V), preferred_element_type=F32)
    lane = lax.broadcasted_iota(jnp.int32, (pieces, 128), 1)
    for t in range(8):
        for tile in range(4):
            rows = [
                by_occ[(OB * t + k) * 16 : (OB * t + k) * 16 + 16, tile * 128 : tile * 128 + 128]
                for k in range(OB)
            ]
            for q in range(4):
                moved = [
                    r if k == q else pltpu.roll(r, (32 * (k - q)) % 128, 1)
                    for k, r in enumerate(rows)
                ]
                block = jnp.where(lane < 32, moved[0], jnp.where(lane < 64, moved[1], jnp.where(lane < 96, moved[2], 0.0))).astype(BF16)
                s = tile * 4 + q
                send[t * 16 + s, :, 0:128] = block
                send[(s // 2) * 16 + t * 2 + s % 2, :, 128:256] = block
    mine = got_ref.at[pl.ds(me * 16, 16)]
    own = pltpu.make_async_copy(send.at[me], mine, recv_sem)
    own.start()
    z, y, x, core = ia >> 1, (ia & 1) * 2 + aux, ja >> 1, ja & 1

    def one(step_, carry):
        o = (step_ * 37) & 127
        dz = (z + (o >> 5)) & 3
        dy = (y + (o >> 3)) & 3
        dx = (x + (o >> 1)) & 3
        dc = (core + o) & 1
        tia, tja, taux = dz * 2 + (dy >> 1), dx * 2 + dc, dy & 1
        pltpu.make_async_remote_copy(
            src_ref=send.at[tia * 16 + tja * 2 + taux], dst_ref=mine,
            send_sem=send_sem, recv_sem=recv_sem,
            device_id={"ia": tia, "ja": tja, "aux": taux}, device_id_type=MESH,
        ).start()
        return carry

    lax.fori_loop(1, 128, one, 0)
    pltpu.make_async_copy(send, send, recv_sem).wait()
    pltpu.make_async_copy(send.at[pl.ds(0, 127)], send.at[pl.ds(0, 127)], send_sem).wait()


def body(raw_integrals, metric_root, eps_occ, eps_vir):
    aux_index = lax.axis_index("aux")
    pieces = raw_integrals.shape[0]
    aux_total = metric_root.shape[0]
    got = pl.pallas_call(
        spread_kernel,
        out_shape=jax.ShapeDtypeStruct((aux_total, 256), BF16),
        in_specs=[pl.BlockSpec(memory_space=pltpu.VMEM)],
        out_specs=pl.BlockSpec(memory_space=pltpu.VMEM),
        scratch_shapes=[
            pltpu.VMEM((128, pieces, 256), BF16),
            pltpu.SemaphoreType.DMA,
            pltpu.SemaphoreType.DMA,
            pltpu.SemaphoreType.DMA,
        ],
        compiler_params=pltpu.CompilerParams(has_side_effects=True),
    )(raw_integrals)
    ev_half = lax.dynamic_slice_in_dim(eps_vir, aux_index * HALF, HALF, 0)
    vmem = pl.BlockSpec(memory_space=pltpu.VMEM)
    out = pl.pallas_call(
        kernel,
        out_shape=jax.ShapeDtypeStruct((OB, HALF, HALF), F32),
        in_specs=[
            vmem,
            pl.BlockSpec(memory_space=pl.ANY),
            pl.BlockSpec(memory_space=pltpu.SMEM),
            vmem,
            vmem,
        ],
        out_specs=vmem,
        scratch_shapes=[
            pltpu.VMEM((NC, OB, 4, 2, 2, 32, QC), BF16),
            pltpu.VMEM((NC, OB, 4, 4, 32, QC), BF16),
            pltpu.VMEM((NC, aux_total, QC), BF16),
            pltpu.VMEM((OB, OB, HALF, V), F32),
            pltpu.VMEM((OB, HALF, OB * V), BF16),
            pltpu.VMEM((4, ROWS, HALF), F32),
            pltpu.VMEM((4, ROWS, HALF), BF16),
            pltpu.VMEM((4, ROWS, HALF), BF16),
            pltpu.VMEM((ROWS, HALF), BF16),
            pltpu.VMEM((ROWS, HALF), BF16),
            pltpu.VMEM((2, ROWS, HALF), BF16),
            pltpu.VMEM((2, ROWS, HALF), BF16),
            pltpu.SemaphoreType.DMA((NC,)),
            pltpu.SemaphoreType.DMA((NC, 25)),
            pltpu.SemaphoreType.DMA((NC, 25)),
            pltpu.SemaphoreType.DMA((10,)),
            pltpu.SemaphoreType.DMA((10,)),
        ],
        compiler_params=pltpu.CompilerParams(
            collective_id=0, has_side_effects=True, vmem_limit_bytes=60 * 2**20
        ),
    )(got, metric_root, eps_occ, eps_vir.reshape(1, V), ev_half.reshape(HALF, 1))
    return out.transpose(1, 0, 2)


def solution(mesh):
    in_specs = (P(("ia", "ja", "aux"), None, None), P(), P(), P())
    out_specs = P("ja", "ia", "aux")
    return jax.shard_map(body, mesh=mesh, in_specs=in_specs, out_specs=out_specs, check_vma=False)
```

```python
import jax
import jax.numpy as jnp
from jax import lax
from jax.experimental import pallas as pl
from jax.experimental.pallas import tpu as pltpu
from jax.sharding import PartitionSpec as P

OB = 3
V = 512
NC = 4
QC = 512
HALF = 256
ROWS = OB * HALF
F32 = jnp.float32
BF16 = jnp.bfloat16
MESH = pl.DeviceIdType.MESH
GROUPS = (
    (0, 0, 128, 128),
    (0, 256, 128, 128),
    (1, 0, 384, 128),
    (2, 0, 256, 256),
    (3, 0, 128, 128),
    (3, 256, 128, 128),
)
PASSES = ((0, 0, 512), (1, 0, 512), (2, 0, 512), (3, 0, 256), (3, 256, 256))
SEQ = (
    ("j0", 0), ("j0", 1), ("j1a", 0), ("j1b", 0), ("j0", 2), ("j1c", 0), ("i1", 0), ("j1a", 1), ("j0", 4),
    ("j1c", 1), ("j1d", 0), ("i1", 1), ("j1d", 1), ("j1b", 1), ("j2a", 0), ("j1a", 2), ("j0", 3), ("j1c", 4),
    ("j1b", 2), ("j1d", 4), ("i2b", 0), ("j1d", 2), ("j1c", 2), ("j2b", 0), ("i1", 2), ("j2a", 1), ("j2b", 1),
    ("i2a", 0), ("j3a", 0), ("i2b", 1), ("j1b", 4), ("j1b", 3), ("i2a", 1), ("j3b", 0), ("j1c", 3),
    ("j1d", 3), ("j2a", 2), ("j1a", 3), ("j0", 5), ("i1", 3), ("j3a", 1), ("j2b", 2), ("j3c", 0), ("j3d", 0),
    ("j3b", 1), ("j3c", 1), ("j3d", 1), ("j1b", 5), ("j2a", 3), ("i1", 4), ("j1a", 4), ("j1a", 5), ("j2b", 3),
    ("i3", 0), ("i1", 5), ("i3", 1), ("j1c", 5), ("j4", 0), ("i2b", 3), ("j2b", 4), ("i2a", 3), ("j3c", 2),
    ("i4", 1), ("i2a", 2), ("j3a", 2), ("j1d", 5), ("j3d", 2), ("j4", 1), ("j2a", 4), ("i4", 0), ("i2b", 2),
    ("co0", 0), ("j3b", 2), ("co1", 0), ("j3b", 3), ("j2b", 5), ("i2b", 4), ("i2a", 4), ("i2a", 5),
    ("j2a", 5), ("j3c", 3), ("i3", 3), ("i2b", 5), ("j3a", 3), ("j3d", 3), ("i3", 2), ("i4", 3), ("j3b", 4),
    ("i3", 4), ("j3c", 4), ("j3d", 4), ("i4", 2), ("j4", 2), ("co0", 1), ("i3", 5), ("j3a", 4), ("co1", 1),
    ("j3a", 5), ("i4", 4), ("j3c", 5), ("i4", 5), ("j3d", 5), ("j4", 3), ("co0", 2), ("j3b", 5), ("co1", 2),
    ("j4", 4), ("co0", 3), ("co1", 3), ("j4", 5),
)
NG = len(GROUPS)


def kernel(
    raw_hbm, met_hbm, eocc_hbm, ev_hbm, out_hbm,
    raw_ref, eocc_ref, ev_ref, blocks, send, got, flat, evc, rden, fi, fj, met, acc, amp, gown, sib_s, sib_r, opp_s, opp_r, rs_s, rs_r, out_ref,
    met_sem, in_sem, all_s, all_r, ss, rs, gs, gr, out_sem,
):
    ia = lax.axis_index("ia")
    ja = lax.axis_index("ja")
    aux = lax.axis_index("aux")
    me = ia * 16 + ja * 2 + aux
    z, yh = ia >> 1, ia & 1
    x, core = ja >> 1, ja & 1
    y = yh * 2 + aux
    other = 1 - core

    def place(index):
        return {"ia": index >> 4, "ja": (index >> 1) & 7, "aux": index & 1}

    def step(v, d):
        return (v + (d + 4)) & 3

    def ydev(d):
        w = step(y, d)
        return {"ia": z * 2 + (w >> 1), "ja": ja, "aux": w & 1}

    def zdev(d):
        return {"ia": step(z, d) * 2 + yh, "ja": ja, "aux": aux}

    def xdev(d):
        return {"ia": ia, "ja": step(x, d) * 2 + core, "aux": aux}

    sib = {"ia": ia, "ja": x * 2 + other, "aux": aux}
    ypart = {"ia": ia, "ja": ja, "aux": 1 - aux}

    barrier = pltpu.get_barrier_semaphore()

    inputs = [
        pltpu.make_async_copy(raw_hbm, raw_ref, in_sem.at[0]),
        pltpu.make_async_copy(eocc_hbm, eocc_ref, in_sem.at[1]),
        pltpu.make_async_copy(ev_hbm, ev_ref, in_sem.at[2]),
    ]
    for copy in inputs:
        copy.start()

    def greet(i, carry):
        pl.semaphore_signal(barrier, inc=1, device_id=place(me ^ (127 - i)), device_id_type=MESH)
        return carry

    lax.fori_loop(0, 127, greet, 0)
    met_copies = [
        pltpu.make_async_copy(met_hbm.at[:, pl.ds(c * QC, QC)], met.at[c], met_sem.at[c])
        for c in range(NC)
    ]
    for c in range(NC):
        met_copies[c].start()

    for copy in inputs:
        copy.wait()
    pieces, occ = raw_ref.shape[0], raw_ref.shape[1]
    n = pieces * occ
    row = lax.broadcasted_iota(jnp.int32, (n, n), 0)
    col = lax.broadcasted_iota(jnp.int32, (n, n), 1)
    pick = ((row & 15) * occ + (row >> 4) == col).astype(F32).astype(BF16)
    by_occ = jnp.dot(pick, raw_ref[...].reshape(n, V), preferred_element_type=F32)
    lane = lax.broadcasted_iota(jnp.int32, (pieces, 128), 1)
    for t in range(8):
        for tile in range(4):
            rows = [
                by_occ[(OB * t + k) * 16 : (OB * t + k) * 16 + 16, tile * 128 : tile * 128 + 128]
                for k in range(OB)
            ]
            for q in range(4):
                a, b, c = [
                    r if k == q else pltpu.roll(r, (32 * (k - q)) % 128, 1)
                    for k, r in enumerate(rows)
                ]
                blocks[t * 16 + tile * 4 + q] = jnp.where(
                    lane < 32, a, jnp.where(lane < 64, b, jnp.where(lane < 96, c, 0.0))
                )
    for there in range(128):
        row_part = blocks[there]
        col_part = pltpu.roll(blocks[((there >> 1) & 7) * 16 + (there >> 4) * 2 + (there & 1)], 96, 1)
        upper = jnp.where(lane < 96, row_part, col_part)
        lower = jnp.where(lane[:8] < 64, col_part[:8], pltpu.roll(col_part[8:], 64, 1))
        send[there] = jnp.concatenate([upper, lower], axis=0).astype(BF16)

    pl.semaphore_wait(barrier, 127)
    mine = got.at[me]
    pltpu.make_async_copy(send.at[me], mine, all_r).start()

    def one(i, carry):
        there = me ^ (128 - i)
        pltpu.make_async_remote_copy(
            src_ref=send.at[there], dst_ref=mine, send_sem=all_s, recv_sem=all_r,
            device_id=place(there), device_id_type=MESH,
        ).start()
        return carry

    lax.fori_loop(1, 128, one, 0)

    for j in range(2):
        lanes = pl.ds(pl.multiple_of(aux * HALF + j * 128, 128), 128)
        evc[j * 128 : (j + 1) * 128] = jnp.broadcast_to(ev_ref[:, lanes], (128, 128)).T

    def invert(p, carry):
        k, l = lax.div(p, OB), lax.rem(p, OB)
        ei, ej = eocc_ref[OB * ia + k], eocc_ref[OB * ja + l]
        for tile in range(4):
            lanes = slice(tile * 128, tile * 128 + 128)
            rden[k, l, :, lanes] = 1.0 / (evc[...] + ev_ref[:, lanes] - ei - ej)
        return carry

    lax.fori_loop(0, OB * OB, invert, 0)

    def put(ref, g, i, dev):
        pltpu.make_async_remote_copy(
            src_ref=ref, dst_ref=ref, send_sem=ss.at[g, int(i > 12)], recv_sem=rs.at[g, i],
            device_id=dev, device_id_type=MESH,
        ).start()

    def arrived(ref, g, i):
        pltpu.make_async_copy(ref, ref, rs.at[g, i]).wait()

    every = slice(None)
    lo, hi = pl.ds(0, 16), pl.ds(16, 16)
    first2, last2 = pl.ds(0, 2), pl.ds(2, 2)
    yp, ym, y2 = step(y, 1), step(y, -1), step(y, 2)
    zp, zm, z2 = step(z, 1), step(z, -1), step(z, 2)
    xp, xm, x2 = step(x, 1), step(x, -1), step(x, 2)

    def fja(g, zz, yy, r=every):
        c, start, na, nb = GROUPS[g]
        return fj.at[c, :, zz, yy, r, pl.ds(start, na)]

    def fjb(g, zz, yy, r=every):
        c, start, na, nb = GROUPS[g]
        return fj.at[c, :, zz, yy, r, pl.ds(start + na, nb)]

    def fig(g, xx, cc, aa=every):
        c, start, na, nb = GROUPS[g]
        return fi.at[c, :, xx, cc, aa, :, pl.ds(start, na + nb)]

    def received():
        pltpu.make_async_copy(send, send, all_r).wait()
        for h in range(4):
            sources = slice(h * 32, h * 32 + 32)
            cells = got[sources].astype(F32)
            lower = cells[:, 16:24]
            rest = jnp.concatenate([lower, pltpu.roll(lower, 64, 2)], axis=1)
            lanes = slice(h * 512, h * 512 + 512)
            flat[0:128, lanes] = cells[:, 0:16].reshape(512, 128).astype(BF16).T
            flat[128:192, lanes] = rest.reshape(512, 128).astype(BF16).T[0:64]

    waited = set()

    def fit(g):
        c, start, na, nb = GROUPS[g]
        if c not in waited:
            met_copies[c].wait()
            waited.add(c)
        lanes = slice(start, start + na + nb)
        r = jnp.dot(flat[...], met[c, :, lanes], preferred_element_type=F32).astype(BF16)
        for k in range(OB):
            fi[c, k, x, core, aux, :, lanes] = r[32 * k : 32 * k + 32]
            fj[c, k, z, y, :, lanes] = r[96 + 32 * k : 128 + 32 * k]

    lone_src, lone_dst = (y + 1 + 2 * aux) & 3, (y + 3 + 2 * aux) & 3
    lone = {"ia": z * 2 + (lone_dst >> 1), "ja": ja, "aux": lone_dst & 1}
    middle2 = pl.ds(1, 2)

    def j0(g):
        fit(g)
        put(fja(g, z, y), g, 0, ydev(1))
        put(fja(g, z, y), g, 1, ydev(-1))
        put(fjb(g, z, y), g, 2, zdev(1))
        put(fjb(g, z, y), g, 3, zdev(-1))
        put(fig(g, x, core, aux), g, 13, ypart)

    def i1(g):
        arrived(fig(g, x, core, 1 - aux), g, 13)
        put(fig(g, x, core), g, 14, xdev(1))
        put(fig(g, x, core), g, 15, xdev(-1))
        put(fig(g, x, core), g, 17, sib)

    def j1a(g):
        arrived(fja(g, z, ym), g, 0)
        put(fja(g, z, ym, lo), g, 5, ydev(1))

    def j1b(g):
        arrived(fja(g, z, yp), g, 1)
        put(fja(g, z, yp, hi), g, 5, ydev(-1))

    def j1c(g):
        arrived(fjb(g, zm, y), g, 2)
        put(fjb(g, zm, y, lo), g, 6, zdev(1))

    def j1d(g):
        arrived(fjb(g, zp, y), g, 3)
        put(fjb(g, zp, y, hi), g, 6, zdev(-1))

    def j2a(g):
        arrived(fja(g, z, y2), g, 5)
        put(fja(g, z, every), g, 7, zdev(1))
        put(fja(g, z, every), g, 8, zdev(-1))

    def j2b(g):
        arrived(fjb(g, z2, y), g, 6)
        put(fjb(g, every, y), g, 9, ydev(1))
        put(fjb(g, every, y), g, 10, ydev(-1))

    def i2a(g):
        arrived(fig(g, xm, core), g, 14)
        put(fig(g, xm, core, 0), g, 16, xdev(1))
        put(fig(g, xm, core), g, 17, sib)

    def i2b(g):
        arrived(fig(g, xp, core), g, 15)
        put(fig(g, xp, core, 1), g, 16, xdev(-1))
        put(fig(g, xp, core), g, 17, sib)

    def j3a(g):
        arrived(fja(g, zm, every), g, 7)
        put(fja(g, zm, first2), g, 11, zdev(1))

    def j3b(g):
        arrived(fja(g, zp, every), g, 8)
        put(fja(g, zp, last2), g, 11, zdev(-1))

    def j3c(g):
        arrived(fjb(g, every, ym), g, 9)
        put(fjb(g, 0, ym), g, 12, ydev(1))

    def j3d(g):
        arrived(fjb(g, every, yp), g, 10)
        put(fjb(g, 3, yp), g, 12, ydev(-1))
        put(fjb(g, middle2, lone_src), g, 12, lone)

    def i3(g):
        arrived(fig(g, x2, core), g, 16)
        put(fig(g, x2, core), g, 17, sib)

    def i4(g):
        arrived(fig(g, every, other), g, 17)

    def j4(g):
        arrived(fja(g, z2, every), g, 11)
        arrived(fjb(g, every, y2), g, 12)

    over_q = (((1,), (1,)), ((), ()))

    half = pl.ds(2 * aux, 2)

    def direct(p):
        c, start, width = PASSES[p]
        lanes = slice(start, start + width)

        def one(l, carry):
            part = lax.dot_general(
                fi[c, :, half, :, :, :, lanes].reshape(ROWS, width),
                fj[c, l, :, :, :, lanes].reshape(V, width),
                over_q,
                preferred_element_type=F32,
            )
            for k in range(OB):
                value = 2.0 * part[k * HALF : (k + 1) * HALF]
                acc[k, l] = value if p == 0 else acc[k, l] + value
            return carry

        lax.fori_loop(0, OB, one, 0)

    def swapped(p, k):
        c, start, width = PASSES[p]
        lanes = slice(start, start + width)
        return lax.dot_general(
            fj[c, :, half, :, :, lanes].reshape(ROWS, width),
            fi[c, k, :, :, :, :, lanes].reshape(V, width),
            over_q,
            preferred_element_type=F32,
        )

    def swap(p):
        def one(k, carry):
            part = swapped(p, k)
            for l in range(OB):
                acc[k, l] = acc[k, l] - part[l * HALF : (l + 1) * HALF]
            return carry

        lax.fori_loop(0, OB, one, 0)

    steps = dict(
        j0=j0, i1=i1, j1a=j1a, j1b=j1b, j1c=j1c, j1d=j1d, j2a=j2a, j2b=j2b, i2a=i2a, i2b=i2b,
        j3a=j3a, j3b=j3b, j3c=j3c, j3d=j3d, i3=i3, i4=i4, j4=j4, co0=direct, co1=swap,
    )
    received()
    for name, g in SEQ:
        steps[name](g)

    def send_to(src, dst, kind, i, dev):
        pltpu.make_async_remote_copy(
            src_ref=src, dst_ref=dst, send_sem=gs.at[kind], recv_sem=gr.at[i],
            device_id=dev, device_id_type=MESH,
        ).start()

    def landed(dst, i):
        pltpu.make_async_copy(dst, dst, gr.at[i]).wait()

    plus, minus = pl.ds(0, 128), pl.ds(128, 128)
    rows_of = [pl.ds(k * HALF, HALF) for k in range(OB)]

    def amplitude(k):
        part = swapped(len(PASSES) - 1, k)
        for l in range(OB):
            value = (acc[k, l] - part[l * HALF : (l + 1) * HALF]) * rden[k, l]
            amp[k, :, l * V : (l + 1) * V] = value.astype(BF16)

    def gamma(m, block, ks, r, i):
        total = None
        for l in range(OB):
            value = jnp.dot(
                amp[ks, :, l * V : (l + 1) * V].reshape(-1, V),
                fj[block, l].reshape(V, QC),
                preferred_element_type=F32,
            )
            total = value if total is None else total + value
        low, high = total[:, :HALF], total[:, HALF:]
        sib_s[m, r] = jnp.where(core == 0, high, low).astype(BF16)
        send_to(sib_s.at[m, r], sib_r.at[m, r], 0, i, sib)
        gown[m, r] = jnp.where(core == 0, low, high)

    def near(m, k, block):
        gamma(m, block, slice(k, k + 1), rows_of[k], 3 * m + k)

    def far_send(k):
        r = rows_of[k]
        landed(sib_r.at[0, r], k)
        opp_s[r] = (gown[0, r] + sib_r[0, r].astype(F32)).astype(BF16)
        send_to(opp_s.at[r, plus], opp_r.at[r, plus], 1, 10 + k, xdev(1))
        send_to(opp_s.at[r, minus], opp_r.at[r, minus], 1, 13 + k, xdev(-1))

    def free(m, k):
        r, lanes, dev = rows_of[k], (minus, plus)[m - 1], xdev((1, -1)[m - 1])
        landed(sib_r.at[m, r], 3 * m + k)
        gown[m, r] = gown[m, r] + sib_r[m, r].astype(F32)
        rs_s[m - 1, r, lanes] = gown[m, r, lanes].astype(BF16)
        send_to(rs_s.at[m - 1, r, lanes], rs_r.at[m - 1, r, lanes], 2, 16 + k, dev)

    def relay(m, k):
        r, lanes, dev = rows_of[k], (plus, minus)[m - 1], xdev((1, -1)[m - 1])
        landed(opp_r.at[r, lanes], (10, 13)[m - 1] + k)
        rs_s[m - 1, r, lanes] = (gown[m, r, lanes] + opp_r[r, lanes].astype(F32)).astype(BF16)
        send_to(rs_s.at[m - 1, r, lanes], rs_r.at[m - 1, r, lanes], 2, 16 + k, dev)

    direct(len(PASSES) - 1)
    amplitude(0)
    near(0, 0, x2)
    near(1, 0, xp)
    far_send(0)
    near(2, 0, xm)
    free(1, 0)
    amplitude(1)
    near(0, 1, x2)
    free(2, 0)
    near(1, 1, xp)
    far_send(1)
    relay(1, 0)
    relay(2, 0)
    near(2, 1, xm)
    free(1, 1)
    amplitude(2)
    near(0, 2, x2)
    free(2, 1)
    near(1, 2, xp)
    far_send(2)
    relay(1, 1)
    relay(2, 1)
    near(2, 2, xm)
    free(1, 2)
    gamma(3, x, every, every, 9)
    free(2, 2)
    relay(1, 2)
    relay(2, 2)
    landed(sib_r.at[3], 9)
    gown[3] = gown[3] + sib_r[3].astype(F32)
    results = []
    for k in range(OB):
        r = rows_of[k]
        landed(rs_r.at[:, r], 16 + k)
        total = gown[3, r] + rs_r[0, r].astype(F32) + rs_r[1, r].astype(F32)
        for h in range(2):
            q = pl.ds(h * 128, 128)
            out_ref[k, q] = total[:, h * 128 : (h + 1) * 128].T
            results.append(pltpu.make_async_copy(out_ref.at[k, q], out_hbm.at[k, q], out_sem.at[k, h]))
            results[-1].start()
    def sent(rows, sem):
        size = met.at[0, pl.ds(0, rows)]
        pltpu.make_async_copy(size, size, sem).wait()

    for g in range(NG):
        for kind in range(2):
            sent(45 * (GROUPS[g][2] + GROUPS[g][3]) // 16, ss.at[g, kind])
    for kind, rows in enumerate((2 * ROWS, ROWS // 2, ROWS)):
        sent(rows, gs.at[kind])
    for copy in results:
        copy.wait()
    left = send.at[pl.ds(0, 127)]
    pltpu.make_async_copy(left, left, all_s).wait()


def body(raw_integrals, metric_root, eps_occ, eps_vir):
    pieces = raw_integrals.shape[0]
    aux_total = metric_root.shape[0]
    out = pl.pallas_call(
        kernel,
        out_shape=jax.ShapeDtypeStruct((OB, HALF, HALF), F32),
        in_specs=[pl.BlockSpec(memory_space=pltpu.HBM)] * 4,
        out_specs=pl.BlockSpec(memory_space=pltpu.HBM),
        scratch_shapes=[
            pltpu.VMEM(raw_integrals.shape, BF16),
            pltpu.SMEM(eps_occ.shape, F32),
            pltpu.VMEM((1, V), F32),
            pltpu.VMEM((128, pieces, 128), F32),
            pltpu.VMEM((128, 24, 128), BF16),
            pltpu.VMEM((128, 24, 128), BF16),
            pltpu.VMEM((192, aux_total), BF16),
            pltpu.VMEM((HALF, 128), F32),
            pltpu.VMEM((OB, OB, HALF, V), F32),
            pltpu.VMEM((NC, OB, 4, 2, 2, 32, QC), BF16),
            pltpu.VMEM((NC, OB, 4, 4, 32, QC), BF16),
            pltpu.VMEM((NC, aux_total, QC), BF16),
            pltpu.VMEM((OB, OB, HALF, V), F32),
            pltpu.VMEM((OB, HALF, OB * V), BF16),
            pltpu.VMEM((4, ROWS, HALF), F32),
            pltpu.VMEM((4, ROWS, HALF), BF16),
            pltpu.VMEM((4, ROWS, HALF), BF16),
            pltpu.VMEM((ROWS, HALF), BF16),
            pltpu.VMEM((ROWS, HALF), BF16),
            pltpu.VMEM((2, ROWS, HALF), BF16),
            pltpu.VMEM((2, ROWS, HALF), BF16),
            pltpu.VMEM((OB, HALF, HALF), F32),
            pltpu.SemaphoreType.DMA((NC,)),
            pltpu.SemaphoreType.DMA((3,)),
            pltpu.SemaphoreType.DMA,
            pltpu.SemaphoreType.DMA,
            pltpu.SemaphoreType.DMA((NG, 2)),
            pltpu.SemaphoreType.DMA((NG, 18)),
            pltpu.SemaphoreType.DMA((3,)),
            pltpu.SemaphoreType.DMA((19,)),
            pltpu.SemaphoreType.DMA((OB, 2)),
        ],
        compiler_params=pltpu.CompilerParams(
            collective_id=0, has_side_effects=True, vmem_limit_bytes=60 * 1024 * 1024
        ),
    )(raw_integrals, metric_root, eps_occ, eps_vir.reshape(1, V))
    return out.transpose(1, 0, 2)


def solution(mesh):
    in_specs = (P(("ia", "ja", "aux"), None, None), P(), P(), P())
    out_specs = P("ja", "ia", "aux")
    return jax.shard_map(body, mesh=mesh, in_specs=in_specs, out_specs=out_specs, check_vma=False)
```

```python
import jax
import jax.numpy as jnp
from jax import lax
from jax.experimental import pallas as pl
from jax.experimental.pallas import tpu as pltpu
from jax.sharding import PartitionSpec as P

OB = 3
V = 512
NC = 4
QC = 512
HALF = 256
ROWS = OB * HALF
F32 = jnp.float32
BF16 = jnp.bfloat16
MESH = pl.DeviceIdType.MESH
GROUPS = (
    (0, 0, 128, 128),
    (0, 256, 128, 128),
    (1, 0, 384, 128),
    (2, 0, 256, 256),
    (3, 0, 128, 128),
    (3, 256, 128, 128),
)
PASSES = ((0, 0, 256), (0, 256, 256), (1, 0, 512), (2, 0, 512), (3, 0, 256), (3, 256, 256))
SEQ = (
    ("j0", 0), ("j0", 1), ("j1a", 0), ("j1b", 0), ("j0", 2), ("j1c", 0), ("j1b", 1), ("i1", 0), ("j1d", 0),
    ("j1c", 1), ("j1d", 1), ("j1a", 1), ("j0", 4), ("j2a", 0), ("j1a", 2), ("j1b", 2), ("j1c", 2), ("j1d", 2),
    ("j0", 3), ("j2b", 0), ("i1", 1), ("j0", 5), ("j1c", 4), ("j1d", 4), ("j2a", 1), ("i1", 2), ("j1c", 3),
    ("j3b", 0), ("i2b", 0), ("j1b", 3), ("j1d", 5), ("j1b", 4), ("j1d", 3), ("j2a", 2), ("j1a", 3),
    ("j2b", 2), ("i2a", 0), ("j2b", 1), ("j1b", 5), ("i1", 4), ("j3a", 0), ("j3c", 0), ("i1", 3), ("j3d", 0),
    ("j1a", 4), ("j2b", 3), ("j2a", 3), ("j3c", 2), ("i2b", 4), ("j1a", 5), ("j3d", 2), ("i2b", 2),
    ("j3b", 2), ("i2a", 2), ("j1c", 5), ("j3a", 2), ("j4", 0), ("i3", 0), ("j3b", 1), ("j3c", 1), ("i2a", 1),
    ("i2b", 1), ("j3d", 1), ("i2a", 4), ("i2a", 3), ("j3a", 1), ("i2b", 3), ("i4", 0), ("j2b", 4), ("co0", 0),
    ("j2a", 4), ("co1", 0), ("j2b", 5), ("j3b", 3), ("i3", 1), ("j3c", 3), ("j4", 2), ("i3", 2), ("i1", 5),
    ("j3a", 3), ("j3d", 3), ("j2a", 5), ("i3", 4), ("j4", 1), ("i4", 1), ("co0", 1), ("i3", 3), ("co1", 1),
    ("j3c", 4), ("i4", 2), ("co0", 2), ("j3b", 4), ("j3a", 4), ("j3d", 4), ("co1", 2), ("j3c", 5), ("i4", 3),
    ("j3d", 5), ("i2a", 5), ("i2b", 5), ("j4", 3), ("co0", 3), ("j3b", 5), ("j3a", 5), ("co1", 3), ("i4", 4),
    ("j4", 4), ("i3", 5), ("co0", 4), ("co1", 4), ("i4", 5), ("j4", 5),
)
NG = len(GROUPS)


def kernel(
    raw_hbm, met_hbm, eocc_hbm, ev_hbm, out_hbm,
    raw_ref, eocc_ref, ev_ref, blocks, send, got, flat, evc, rden, fi, fj, met, acc, amp, gown, sib_s, sib_r, opp_s, opp_r, rs_s, rs_r, out_ref,
    met_sem, in_sem, all_s, all_r, ss, rs, gs, gr, out_sem,
):
    ia = lax.axis_index("ia")
    ja = lax.axis_index("ja")
    aux = lax.axis_index("aux")
    me = ia * 16 + ja * 2 + aux
    z, yh = ia >> 1, ia & 1
    x, core = ja >> 1, ja & 1
    y = yh * 2 + aux
    other = 1 - core

    def place(index):
        return {"ia": index >> 4, "ja": (index >> 1) & 7, "aux": index & 1}

    def step(v, d):
        return (v + (d + 4)) & 3

    def ydev(d):
        w = step(y, d)
        return {"ia": z * 2 + (w >> 1), "ja": ja, "aux": w & 1}

    def zdev(d):
        return {"ia": step(z, d) * 2 + yh, "ja": ja, "aux": aux}

    def xdev(d):
        return {"ia": ia, "ja": step(x, d) * 2 + core, "aux": aux}

    sib = {"ia": ia, "ja": x * 2 + other, "aux": aux}
    ypart = {"ia": ia, "ja": ja, "aux": 1 - aux}

    barrier = pltpu.get_barrier_semaphore()

    inputs = [
        pltpu.make_async_copy(raw_hbm, raw_ref, in_sem.at[0]),
        pltpu.make_async_copy(eocc_hbm, eocc_ref, in_sem.at[1]),
        pltpu.make_async_copy(ev_hbm, ev_ref, in_sem.at[2]),
    ]
    for copy in inputs:
        copy.start()

    for o in range(127, 0, -1):
        pl.semaphore_signal(barrier, inc=1, device_id=me ^ o, device_id_type=pl.DeviceIdType.LOGICAL)
    met_copies = [
        pltpu.make_async_copy(met_hbm.at[:, pl.ds(c * QC, QC)], met.at[c], met_sem.at[c])
        for c in range(NC)
    ]
    for c in range(NC):
        met_copies[c].start()

    for copy in inputs:
        copy.wait()
    pieces, occ = raw_ref.shape[0], raw_ref.shape[1]
    n = pieces * occ
    row = lax.broadcasted_iota(jnp.int32, (n, n), 0)
    col = lax.broadcasted_iota(jnp.int32, (n, n), 1)
    pick = ((row & 15) * occ + (row >> 4) == col).astype(F32).astype(BF16)
    by_occ = jnp.dot(pick, raw_ref[...].reshape(n, V), preferred_element_type=F32)
    lane = lax.broadcasted_iota(jnp.int32, (pieces, 128), 1)
    for t in range(8):
        for tile in range(4):
            rows = [
                by_occ[(OB * t + k) * 16 : (OB * t + k) * 16 + 16, tile * 128 : tile * 128 + 128]
                for k in range(OB)
            ]
            for q in range(4):
                a, b, c = [
                    r if k == q else pltpu.roll(r, (32 * (k - q)) % 128, 1)
                    for k, r in enumerate(rows)
                ]
                blocks[t * 16 + tile * 4 + q] = jnp.where(
                    lane < 32, a, jnp.where(lane < 64, b, jnp.where(lane < 96, c, 0.0))
                )
    for there in range(128):
        row_part = blocks[there]
        col_part = pltpu.roll(blocks[((there >> 1) & 7) * 16 + (there >> 4) * 2 + (there & 1)], 96, 1)
        upper = jnp.where(lane < 96, row_part, col_part)
        lower = jnp.where(lane[:8] < 64, col_part[:8], pltpu.roll(col_part[8:], 64, 1))
        send[there] = jnp.concatenate([upper, lower], axis=0).astype(BF16)

    pl.semaphore_wait(barrier, 127)
    mine = got.at[me]
    pltpu.make_async_copy(send.at[me], mine, all_r).start()

    def one(i, carry):
        there = me ^ ((i * 37) & 127)
        pltpu.make_async_remote_copy(
            src_ref=send.at[there], dst_ref=mine, send_sem=all_s, recv_sem=all_r,
            device_id=there, device_id_type=pl.DeviceIdType.LOGICAL,
        ).start()
        return carry

    lax.fori_loop(1, 128, one, 0)

    for j in range(2):
        lanes = pl.ds(pl.multiple_of(aux * HALF + j * 128, 128), 128)
        evc[j * 128 : (j + 1) * 128] = jnp.broadcast_to(ev_ref[:, lanes], (128, 128)).T

    def invert(p, carry):
        k, l = lax.div(p, OB), lax.rem(p, OB)
        ei, ej = eocc_ref[OB * ia + k], eocc_ref[OB * ja + l]
        for tile in range(4):
            lanes = slice(tile * 128, tile * 128 + 128)
            rden[k, l, :, lanes] = 1.0 / (evc[...] + ev_ref[:, lanes] - ei - ej)
        return carry

    lax.fori_loop(0, OB * OB, invert, 0)

    def put(ref, g, i, dev):
        pltpu.make_async_remote_copy(
            src_ref=ref, dst_ref=ref, send_sem=ss.at[g, int(i > 12)], recv_sem=rs.at[g, i],
            device_id=dev, device_id_type=MESH,
        ).start()

    def arrived(ref, g, i):
        pltpu.make_async_copy(ref, ref, rs.at[g, i]).wait()

    every = slice(None)
    lo, hi = pl.ds(0, 16), pl.ds(16, 16)
    first2, last2 = pl.ds(0, 2), pl.ds(2, 2)
    yp, ym, y2 = step(y, 1), step(y, -1), step(y, 2)
    zp, zm, z2 = step(z, 1), step(z, -1), step(z, 2)
    xp, xm, x2 = step(x, 1), step(x, -1), step(x, 2)

    def fja(g, zz, yy, r=every):
        c, start, na, nb = GROUPS[g]
        return fj.at[c, :, zz, yy, r, pl.ds(start, na)]

    def fjb(g, zz, yy, r=every):
        c, start, na, nb = GROUPS[g]
        return fj.at[c, :, zz, yy, r, pl.ds(start + na, nb)]

    def fig(g, xx, cc, aa=every):
        c, start, na, nb = GROUPS[g]
        return fi.at[c, :, xx, cc, aa, :, pl.ds(start, na + nb)]

    def received():
        pltpu.make_async_copy(send, send, all_r).wait()
        for h in range(4):
            sources = slice(h * 32, h * 32 + 32)
            cells = got[sources].astype(F32)
            lower = cells[:, 16:24]
            rest = jnp.concatenate([lower, pltpu.roll(lower, 64, 2)], axis=1)
            lanes = slice(h * 512, h * 512 + 512)
            flat[0:128, lanes] = cells[:, 0:16].reshape(512, 128).astype(BF16).T
            flat[128:192, lanes] = rest.reshape(512, 128).astype(BF16).T[0:64]

    waited = set()

    def fit(g):
        c, start, na, nb = GROUPS[g]
        if c not in waited:
            met_copies[c].wait()
            waited.add(c)
        lanes = slice(start, start + na + nb)
        r = jnp.dot(flat[...], met[c, :, lanes], preferred_element_type=F32).astype(BF16)
        for k in range(OB):
            fi[c, k, x, core, aux, :, lanes] = r[32 * k : 32 * k + 32]
            fj[c, k, z, y, :, lanes] = r[96 + 32 * k : 128 + 32 * k]

    lone_src, lone_dst = (y + 1 + 2 * aux) & 3, (y + 3 + 2 * aux) & 3
    lone = {"ia": z * 2 + (lone_dst >> 1), "ja": ja, "aux": lone_dst & 1}
    middle2 = pl.ds(1, 2)

    def j0(g):
        fit(g)
        put(fja(g, z, y), g, 0, ydev(1))
        put(fja(g, z, y), g, 1, ydev(-1))
        put(fjb(g, z, y), g, 2, zdev(1))
        put(fjb(g, z, y), g, 3, zdev(-1))
        put(fig(g, x, core, aux), g, 13, ypart)

    def i1(g):
        arrived(fig(g, x, core, 1 - aux), g, 13)
        put(fig(g, x, core), g, 14, xdev(1))
        put(fig(g, x, core), g, 15, xdev(-1))
        put(fig(g, x, core), g, 17, sib)

    def j1a(g):
        arrived(fja(g, z, ym), g, 0)
        put(fja(g, z, ym, lo), g, 5, ydev(1))

    def j1b(g):
        arrived(fja(g, z, yp), g, 1)
        put(fja(g, z, yp, hi), g, 5, ydev(-1))

    def j1c(g):
        arrived(fjb(g, zm, y), g, 2)
        put(fjb(g, zm, y, lo), g, 6, zdev(1))

    def j1d(g):
        arrived(fjb(g, zp, y), g, 3)
        put(fjb(g, zp, y, hi), g, 6, zdev(-1))

    def j2a(g):
        arrived(fja(g, z, y2), g, 5)
        put(fja(g, z, every), g, 7, zdev(1))
        put(fja(g, z, every), g, 8, zdev(-1))

    def j2b(g):
        arrived(fjb(g, z2, y), g, 6)
        put(fjb(g, every, y), g, 9, ydev(1))
        put(fjb(g, every, y), g, 10, ydev(-1))

    def i2a(g):
        arrived(fig(g, xm, core), g, 14)
        put(fig(g, xm, core, 0), g, 16, xdev(1))
        put(fig(g, xm, core), g, 17, sib)

    def i2b(g):
        arrived(fig(g, xp, core), g, 15)
        put(fig(g, xp, core, 1), g, 16, xdev(-1))
        put(fig(g, xp, core), g, 17, sib)

    def j3a(g):
        arrived(fja(g, zm, every), g, 7)
        put(fja(g, zm, first2), g, 11, zdev(1))

    def j3b(g):
        arrived(fja(g, zp, every), g, 8)
        put(fja(g, zp, last2), g, 11, zdev(-1))

    def j3c(g):
        arrived(fjb(g, every, ym), g, 9)
        put(fjb(g, 0, ym), g, 12, ydev(1))

    def j3d(g):
        arrived(fjb(g, every, yp), g, 10)
        put(fjb(g, 3, yp), g, 12, ydev(-1))
        put(fjb(g, middle2, lone_src), g, 12, lone)

    def i3(g):
        arrived(fig(g, x2, core), g, 16)
        put(fig(g, x2, core), g, 17, sib)

    def i4(g):
        arrived(fig(g, every, other), g, 17)

    def j4(g):
        arrived(fja(g, z2, every), g, 11)
        arrived(fjb(g, every, y2), g, 12)

    over_q = (((1,), (1,)), ((), ()))

    half = pl.ds(2 * aux, 2)

    def direct(p):
        c, start, width = PASSES[p]
        lanes = slice(start, start + width)

        for l in range(OB):
            part = lax.dot_general(
                fi[c, :, half, :, :, :, lanes].reshape(ROWS, width),
                fj[c, l, :, :, :, lanes].reshape(V, width),
                over_q,
                preferred_element_type=F32,
            )
            for k in range(OB):
                value = 2.0 * part[k * HALF : (k + 1) * HALF]
                acc[k, l] = value if p == 0 else acc[k, l] + value

    def swapped(p, k):
        c, start, width = PASSES[p]
        lanes = slice(start, start + width)
        return lax.dot_general(
            fj[c, :, half, :, :, lanes].reshape(ROWS, width),
            fi[c, k, :, :, :, :, lanes].reshape(V, width),
            over_q,
            preferred_element_type=F32,
        )

    def swap(p):
        for k in range(OB):
            part = swapped(p, k)
            for l in range(OB):
                acc[k, l] = acc[k, l] - part[l * HALF : (l + 1) * HALF]

    steps = dict(
        j0=j0, i1=i1, j1a=j1a, j1b=j1b, j1c=j1c, j1d=j1d, j2a=j2a, j2b=j2b, i2a=i2a, i2b=i2b,
        j3a=j3a, j3b=j3b, j3c=j3c, j3d=j3d, i3=i3, i4=i4, j4=j4, co0=direct, co1=swap,
    )
    received()
    for name, g in SEQ:
        steps[name](g)

    def send_to(src, dst, kind, i, dev):
        pltpu.make_async_remote_copy(
            src_ref=src, dst_ref=dst, send_sem=gs.at[kind], recv_sem=gr.at[i],
            device_id=dev, device_id_type=MESH,
        ).start()

    def landed(dst, i):
        pltpu.make_async_copy(dst, dst, gr.at[i]).wait()

    plus, minus = pl.ds(0, 128), pl.ds(128, 128)
    rows_of = [pl.ds(k * HALF, HALF) for k in range(OB)]

    def amplitude(k):
        part = swapped(len(PASSES) - 1, k)
        for l in range(OB):
            value = (acc[k, l] - part[l * HALF : (l + 1) * HALF]) * rden[k, l]
            amp[k, :, l * V : (l + 1) * V] = value.astype(BF16)

    def gamma(m, block, ks, r, i):
        total = None
        for l in range(OB):
            value = jnp.dot(
                amp[ks, :, l * V : (l + 1) * V].reshape(-1, V),
                fj[block, l].reshape(V, QC),
                preferred_element_type=F32,
            )
            total = value if total is None else total + value
        low, high = total[:, :HALF], total[:, HALF:]
        sib_s[m, r] = jnp.where(core == 0, high, low).astype(BF16)
        send_to(sib_s.at[m, r], sib_r.at[m, r], 0, i, sib)
        gown[m, r] = jnp.where(core == 0, low, high)

    def near(m, k, block):
        gamma(m, block, slice(k, k + 1), rows_of[k], 3 * m + k)

    def far_send(k):
        r = rows_of[k]
        landed(sib_r.at[0, r], k)
        opp_s[r] = (gown[0, r] + sib_r[0, r].astype(F32)).astype(BF16)
        send_to(opp_s.at[r, plus], opp_r.at[r, plus], 1, 10 + k, xdev(1))
        send_to(opp_s.at[r, minus], opp_r.at[r, minus], 1, 13 + k, xdev(-1))

    def free(m, k):
        r, lanes, dev = rows_of[k], (minus, plus)[m - 1], xdev((1, -1)[m - 1])
        landed(sib_r.at[m, r], 3 * m + k)
        gown[m, r] = gown[m, r] + sib_r[m, r].astype(F32)
        rs_s[m - 1, r, lanes] = gown[m, r, lanes].astype(BF16)
        send_to(rs_s.at[m - 1, r, lanes], rs_r.at[m - 1, r, lanes], 2, 16 + k, dev)

    def relay(m, k):
        r, lanes, dev = rows_of[k], (plus, minus)[m - 1], xdev((1, -1)[m - 1])
        landed(opp_r.at[r, lanes], (10, 13)[m - 1] + k)
        rs_s[m - 1, r, lanes] = (gown[m, r, lanes] + opp_r[r, lanes].astype(F32)).astype(BF16)
        send_to(rs_s.at[m - 1, r, lanes], rs_r.at[m - 1, r, lanes], 2, 16 + k, dev)

    direct(len(PASSES) - 1)
    amplitude(0)
    near(0, 0, x2)
    near(1, 0, xp)
    far_send(0)
    near(2, 0, xm)
    free(1, 0)
    amplitude(1)
    near(0, 1, x2)
    free(2, 0)
    near(1, 1, xp)
    far_send(1)
    relay(1, 0)
    relay(2, 0)
    near(2, 1, xm)
    free(1, 1)
    amplitude(2)
    near(0, 2, x2)
    free(2, 1)
    near(1, 2, xp)
    far_send(2)
    relay(1, 1)
    relay(2, 1)
    near(2, 2, xm)
    free(1, 2)
    gamma(3, x, every, every, 9)
    free(2, 2)
    relay(1, 2)
    relay(2, 2)
    landed(sib_r.at[3], 9)
    gown[3] = gown[3] + sib_r[3].astype(F32)
    results = []
    for k in range(OB):
        r = rows_of[k]
        landed(rs_r.at[:, r], 16 + k)
        total = gown[3, r] + rs_r[0, r].astype(F32) + rs_r[1, r].astype(F32)
        for h in range(2):
            q = pl.ds(h * 128, 128)
            out_ref[k, q] = total[:, h * 128 : (h + 1) * 128].T
            results.append(pltpu.make_async_copy(out_ref.at[k, q], out_hbm.at[k, q], out_sem.at[k, h]))
            results[-1].start()
    def sent(rows, sem):
        size = met.at[0, pl.ds(0, rows)]
        pltpu.make_async_copy(size, size, sem).wait()

    for g in range(NG):
        for kind in range(2):
            sent(45 * (GROUPS[g][2] + GROUPS[g][3]) // 16, ss.at[g, kind])
    for kind, rows in enumerate((2 * ROWS, ROWS // 2, ROWS)):
        sent(rows, gs.at[kind])
    for copy in results:
        copy.wait()
    left = send.at[pl.ds(0, 127)]
    pltpu.make_async_copy(left, left, all_s).wait()


def body(raw_integrals, metric_root, eps_occ, eps_vir):
    pieces = raw_integrals.shape[0]
    aux_total = metric_root.shape[0]
    out = pl.pallas_call(
        kernel,
        out_shape=jax.ShapeDtypeStruct((OB, HALF, HALF), F32),
        in_specs=[pl.BlockSpec(memory_space=pltpu.HBM)] * 4,
        out_specs=pl.BlockSpec(memory_space=pltpu.HBM),
        scratch_shapes=[
            pltpu.VMEM(raw_integrals.shape, BF16),
            pltpu.SMEM(eps_occ.shape, F32),
            pltpu.VMEM((1, V), F32),
            pltpu.VMEM((128, pieces, 128), F32),
            pltpu.VMEM((128, 24, 128), BF16),
            pltpu.VMEM((128, 24, 128), BF16),
            pltpu.VMEM((192, aux_total), BF16),
            pltpu.VMEM((HALF, 128), F32),
            pltpu.VMEM((OB, OB, HALF, V), F32),
            pltpu.VMEM((NC, OB, 4, 2, 2, 32, QC), BF16),
            pltpu.VMEM((NC, OB, 4, 4, 32, QC), BF16),
            pltpu.VMEM((NC, aux_total, QC), BF16),
            pltpu.VMEM((OB, OB, HALF, V), F32),
            pltpu.VMEM((OB, HALF, OB * V), BF16),
            pltpu.VMEM((4, ROWS, HALF), F32),
            pltpu.VMEM((4, ROWS, HALF), BF16),
            pltpu.VMEM((4, ROWS, HALF), BF16),
            pltpu.VMEM((ROWS, HALF), BF16),
            pltpu.VMEM((ROWS, HALF), BF16),
            pltpu.VMEM((2, ROWS, HALF), BF16),
            pltpu.VMEM((2, ROWS, HALF), BF16),
            pltpu.VMEM((OB, HALF, HALF), F32),
            pltpu.SemaphoreType.DMA((NC,)),
            pltpu.SemaphoreType.DMA((3,)),
            pltpu.SemaphoreType.DMA,
            pltpu.SemaphoreType.DMA,
            pltpu.SemaphoreType.DMA((NG, 2)),
            pltpu.SemaphoreType.DMA((NG, 18)),
            pltpu.SemaphoreType.DMA((3,)),
            pltpu.SemaphoreType.DMA((19,)),
            pltpu.SemaphoreType.DMA((OB, 2)),
        ],
        compiler_params=pltpu.CompilerParams(
            collective_id=0, has_side_effects=True, vmem_limit_bytes=60 * 1024 * 1024
        ),
    )(raw_integrals, metric_root, eps_occ, eps_vir.reshape(1, V))
    return out.transpose(1, 0, 2)


def solution(mesh):
    in_specs = (P(("ia", "ja", "aux"), None, None), P(), P(), P())
    out_specs = P("ja", "ia", "aux")
    return jax.shard_map(body, mesh=mesh, in_specs=in_specs, out_specs=out_specs, check_vma=False)
```

```python
import jax
import jax.numpy as jnp
from jax import lax
from jax.experimental import pallas as pl
from jax.experimental.pallas import tpu as pltpu
from jax.sharding import PartitionSpec as P

OB = 3
V = 512
NC = 4
QC = 512
HALF = 256
ROWS = OB * HALF
F32 = jnp.float32
BF16 = jnp.bfloat16
MESH = pl.DeviceIdType.MESH
GROUPS = (
    (0, 0, 128, 128),
    (0, 256, 128, 128),
    (1, 0, 384, 128),
    (2, 0, 256, 256),
    (3, 0, 128, 128),
    (3, 256, 128, 128),
)
PASSES = ((0, 0, 256), (0, 256, 256), (1, 0, 512), (2, 0, 512), (3, 0, 256), (3, 256, 256))
SEQ = (
    ("j0", 0), ("j0", 1), ("j1a", 0), ("j1b", 0), ("j0", 2), ("j1c", 0), ("j1b", 1), ("i1", 0), ("j1d", 0),
    ("j1c", 1), ("j1d", 1), ("j1a", 1), ("j0", 4), ("j2a", 0), ("j1a", 2), ("j1b", 2), ("j1c", 2), ("j1d", 2),
    ("j0", 3), ("j2b", 0), ("i1", 1), ("j0", 5), ("j1c", 4), ("j1d", 4), ("j2a", 1), ("i1", 2), ("j1c", 3),
    ("j3b", 0), ("i2b", 0), ("j1b", 3), ("j1d", 5), ("j1b", 4), ("j1d", 3), ("j2a", 2), ("j1a", 3),
    ("j2b", 2), ("i2a", 0), ("j2b", 1), ("j1b", 5), ("i1", 4), ("j3a", 0), ("j3c", 0), ("i1", 3), ("j3d", 0),
    ("j1a", 4), ("j2b", 3), ("j2a", 3), ("j3c", 2), ("i2b", 4), ("j1a", 5), ("j3d", 2), ("i2b", 2),
    ("j3b", 2), ("i2a", 2), ("j1c", 5), ("j3a", 2), ("j4", 0), ("i3", 0), ("j3b", 1), ("j3c", 1), ("i2a", 1),
    ("i2b", 1), ("j3d", 1), ("i2a", 4), ("i2a", 3), ("j3a", 1), ("i2b", 3), ("i4", 0), ("j2b", 4), ("co0", 0),
    ("j2a", 4), ("co1", 0), ("j2b", 5), ("j3b", 3), ("i3", 1), ("j3c", 3), ("j4", 2), ("i3", 2), ("i1", 5),
    ("j3a", 3), ("j3d", 3), ("j2a", 5), ("i3", 4), ("j4", 1), ("i4", 1), ("co0", 1), ("i3", 3), ("co1", 1),
    ("j3c", 4), ("i4", 2), ("co0", 2), ("j3b", 4), ("j3a", 4), ("j3d", 4), ("co1", 2), ("j3c", 5), ("i4", 3),
    ("j3d", 5), ("i2a", 5), ("i2b", 5), ("j4", 3), ("co0", 3), ("j3b", 5), ("j3a", 5), ("co1", 3), ("i4", 4),
    ("j4", 4), ("i3", 5), ("co0", 4), ("co1", 4), ("i4", 5), ("j4", 5),
)
NG = len(GROUPS)


def kernel(
    raw_hbm, met_hbm, eocc_hbm, ev_hbm, out_hbm,
    raw_ref, eocc_ref, ev_ref, blocks, send, got, flat, evc, rden, fi, fj, met, acc, amp, gown, sib_s, sib_r, opp_s, opp_r, rs_s, rs_r, out_ref,
    met_sem, in_sem, all_s, all_r, ss, rs, gs, gr, out_sem,
):
    ia = lax.axis_index("ia")
    ja = lax.axis_index("ja")
    aux = lax.axis_index("aux")
    me = ia * 16 + ja * 2 + aux
    z, yh = ia >> 1, ia & 1
    x, core = ja >> 1, ja & 1
    y = yh * 2 + aux
    other = 1 - core

    def place(index):
        return {"ia": index >> 4, "ja": (index >> 1) & 7, "aux": index & 1}

    def step(v, d):
        return (v + (d + 4)) & 3

    def ydev(d):
        w = step(y, d)
        return {"ia": z * 2 + (w >> 1), "ja": ja, "aux": w & 1}

    def zdev(d):
        return {"ia": step(z, d) * 2 + yh, "ja": ja, "aux": aux}

    def xdev(d):
        return {"ia": ia, "ja": step(x, d) * 2 + core, "aux": aux}

    sib = {"ia": ia, "ja": x * 2 + other, "aux": aux}
    ypart = {"ia": ia, "ja": ja, "aux": 1 - aux}

    barrier = pltpu.get_barrier_semaphore()

    inputs = [
        pltpu.make_async_copy(raw_hbm, raw_ref, in_sem.at[0]),
        pltpu.make_async_copy(eocc_hbm, eocc_ref, in_sem.at[1]),
        pltpu.make_async_copy(ev_hbm, ev_ref, in_sem.at[2]),
    ]
    for copy in inputs:
        copy.start()

    for o in range(127, 0, -1):
        pl.semaphore_signal(barrier, inc=1, device_id=me ^ o, device_id_type=pl.DeviceIdType.LOGICAL)
    met_copies = [
        pltpu.make_async_copy(met_hbm.at[:, pl.ds(c * QC, QC)], met.at[c], met_sem.at[c])
        for c in range(NC)
    ]
    for c in range(NC):
        met_copies[c].start()

    for copy in inputs:
        copy.wait()
    pieces, occ = raw_ref.shape[0], raw_ref.shape[1]
    n = pieces * occ
    row = lax.broadcasted_iota(jnp.int32, (n, n), 0)
    col = lax.broadcasted_iota(jnp.int32, (n, n), 1)
    pick = ((row & 15) * occ + (row >> 4) == col).astype(F32).astype(BF16)
    by_occ = jnp.dot(pick, raw_ref[...].reshape(n, V), preferred_element_type=F32)
    lane = lax.broadcasted_iota(jnp.int32, (pieces, 128), 1)
    for t in range(8):
        for tile in range(4):
            rows = [
                by_occ[(OB * t + k) * 16 : (OB * t + k) * 16 + 16, tile * 128 : tile * 128 + 128]
                for k in range(OB)
            ]
            for q in range(4):
                a, b, c = [
                    r if k == q else pltpu.roll(r, (32 * (k - q)) % 128, 1)
                    for k, r in enumerate(rows)
                ]
                blocks[t * 16 + tile * 4 + q] = jnp.where(
                    lane < 32, a, jnp.where(lane < 64, b, jnp.where(lane < 96, c, 0.0))
                )
    for there in range(128):
        row_part = blocks[there]
        col_part = pltpu.roll(blocks[((there >> 1) & 7) * 16 + (there >> 4) * 2 + (there & 1)], 96, 1)
        upper = jnp.where(lane < 96, row_part, col_part)
        lower = jnp.where(lane[:8] < 64, col_part[:8], pltpu.roll(col_part[8:], 64, 1))
        send[there] = jnp.concatenate([upper, lower], axis=0).astype(BF16)

    pl.semaphore_wait(barrier, 127)
    mine = got.at[me]
    pltpu.make_async_copy(send.at[me], mine, all_r).start()

    def one(i, carry):
        there = me ^ ((i * 53) & 127)
        pltpu.make_async_remote_copy(
            src_ref=send.at[there], dst_ref=mine, send_sem=all_s, recv_sem=all_r,
            device_id=there, device_id_type=pl.DeviceIdType.LOGICAL,
        ).start()
        return carry

    lax.fori_loop(1, 128, one, 0)

    for j in range(2):
        lanes = pl.ds(pl.multiple_of(aux * HALF + j * 128, 128), 128)
        evc[j * 128 : (j + 1) * 128] = jnp.broadcast_to(ev_ref[:, lanes], (128, 128)).T

    def invert(p, carry):
        k, l = lax.div(p, OB), lax.rem(p, OB)
        ei, ej = eocc_ref[OB * ia + k], eocc_ref[OB * ja + l]
        for tile in range(4):
            lanes = slice(tile * 128, tile * 128 + 128)
            rden[k, l, :, lanes] = 1.0 / (evc[...] + ev_ref[:, lanes] - ei - ej)
        return carry

    lax.fori_loop(0, OB * OB, invert, 0)

    def put(ref, g, i, dev):
        pltpu.make_async_remote_copy(
            src_ref=ref, dst_ref=ref, send_sem=ss.at[g, int(i > 12)], recv_sem=rs.at[g, i],
            device_id=dev, device_id_type=MESH,
        ).start()

    def arrived(ref, g, i):
        pltpu.make_async_copy(ref, ref, rs.at[g, i]).wait()

    every = slice(None)
    lo, hi = pl.ds(0, 16), pl.ds(16, 16)
    first2, last2 = pl.ds(0, 2), pl.ds(2, 2)
    yp, ym, y2 = step(y, 1), step(y, -1), step(y, 2)
    zp, zm, z2 = step(z, 1), step(z, -1), step(z, 2)
    xp, xm, x2 = step(x, 1), step(x, -1), step(x, 2)

    def fja(g, zz, yy, r=every):
        c, start, na, nb = GROUPS[g]
        return fj.at[c, :, zz, yy, r, pl.ds(start, na)]

    def fjb(g, zz, yy, r=every):
        c, start, na, nb = GROUPS[g]
        return fj.at[c, :, zz, yy, r, pl.ds(start + na, nb)]

    def fig(g, xx, cc, aa=every):
        c, start, na, nb = GROUPS[g]
        return fi.at[c, :, xx, cc, aa, :, pl.ds(start, na + nb)]

    def received():
        pltpu.make_async_copy(send, send, all_r).wait()
        for h in range(4):
            sources = slice(h * 32, h * 32 + 32)
            cells = got[sources].astype(F32)
            lower = cells[:, 16:24]
            rest = jnp.concatenate([lower, pltpu.roll(lower, 64, 2)], axis=1)
            lanes = slice(h * 512, h * 512 + 512)
            flat[0:128, lanes] = cells[:, 0:16].reshape(512, 128).astype(BF16).T
            flat[128:192, lanes] = rest.reshape(512, 128).astype(BF16).T[0:64]

    waited = set()

    def fit(g):
        c, start, na, nb = GROUPS[g]
        if c not in waited:
            met_copies[c].wait()
            waited.add(c)
        lanes = slice(start, start + na + nb)
        r = jnp.dot(flat[...], met[c, :, lanes], preferred_element_type=F32).astype(BF16)
        for k in range(OB):
            fi[c, k, x, core, aux, :, lanes] = r[32 * k : 32 * k + 32]
            fj[c, k, z, y, :, lanes] = r[96 + 32 * k : 128 + 32 * k]

    lone_src, lone_dst = (y + 1 + 2 * aux) & 3, (y + 3 + 2 * aux) & 3
    lone = {"ia": z * 2 + (lone_dst >> 1), "ja": ja, "aux": lone_dst & 1}
    middle2 = pl.ds(1, 2)

    def j0(g):
        fit(g)
        put(fja(g, z, y), g, 0, ydev(1))
        put(fja(g, z, y), g, 1, ydev(-1))
        put(fjb(g, z, y), g, 2, zdev(1))
        put(fjb(g, z, y), g, 3, zdev(-1))
        put(fig(g, x, core, aux), g, 13, ypart)

    def i1(g):
        arrived(fig(g, x, core, 1 - aux), g, 13)
        put(fig(g, x, core), g, 14, xdev(1))
        put(fig(g, x, core), g, 15, xdev(-1))
        put(fig(g, x, core), g, 17, sib)

    def j1a(g):
        arrived(fja(g, z, ym), g, 0)
        put(fja(g, z, ym, lo), g, 5, ydev(1))

    def j1b(g):
        arrived(fja(g, z, yp), g, 1)
        put(fja(g, z, yp, hi), g, 5, ydev(-1))

    def j1c(g):
        arrived(fjb(g, zm, y), g, 2)
        put(fjb(g, zm, y, lo), g, 6, zdev(1))

    def j1d(g):
        arrived(fjb(g, zp, y), g, 3)
        put(fjb(g, zp, y, hi), g, 6, zdev(-1))

    def j2a(g):
        arrived(fja(g, z, y2), g, 5)
        put(fja(g, z, every), g, 7, zdev(1))
        put(fja(g, z, every), g, 8, zdev(-1))

    def j2b(g):
        arrived(fjb(g, z2, y), g, 6)
        put(fjb(g, every, y), g, 9, ydev(1))
        put(fjb(g, every, y), g, 10, ydev(-1))

    def i2a(g):
        arrived(fig(g, xm, core), g, 14)
        put(fig(g, xm, core, 0), g, 16, xdev(1))
        put(fig(g, xm, core), g, 17, sib)

    def i2b(g):
        arrived(fig(g, xp, core), g, 15)
        put(fig(g, xp, core, 1), g, 16, xdev(-1))
        put(fig(g, xp, core), g, 17, sib)

    def j3a(g):
        arrived(fja(g, zm, every), g, 7)
        put(fja(g, zm, first2), g, 11, zdev(1))

    def j3b(g):
        arrived(fja(g, zp, every), g, 8)
        put(fja(g, zp, last2), g, 11, zdev(-1))

    def j3c(g):
        arrived(fjb(g, every, ym), g, 9)
        put(fjb(g, 0, ym), g, 12, ydev(1))

    def j3d(g):
        arrived(fjb(g, every, yp), g, 10)
        put(fjb(g, 3, yp), g, 12, ydev(-1))
        put(fjb(g, middle2, lone_src), g, 12, lone)

    def i3(g):
        arrived(fig(g, x2, core), g, 16)
        put(fig(g, x2, core), g, 17, sib)

    def i4(g):
        arrived(fig(g, every, other), g, 17)

    def j4(g):
        arrived(fja(g, z2, every), g, 11)
        arrived(fjb(g, every, y2), g, 12)

    over_q = (((1,), (1,)), ((), ()))

    half = pl.ds(2 * aux, 2)

    def direct(p):
        c, start, width = PASSES[p]
        lanes = slice(start, start + width)

        for l in range(OB):
            part = lax.dot_general(
                fi[c, :, half, :, :, :, lanes].reshape(ROWS, width),
                fj[c, l, :, :, :, lanes].reshape(V, width),
                over_q,
                preferred_element_type=F32,
            )
            for k in range(OB):
                value = 2.0 * part[k * HALF : (k + 1) * HALF]
                acc[k, l] = value if p == 0 else acc[k, l] + value

    def swapped(p, k):
        c, start, width = PASSES[p]
        lanes = slice(start, start + width)
        return lax.dot_general(
            fj[c, :, half, :, :, lanes].reshape(ROWS, width),
            fi[c, k, :, :, :, :, lanes].reshape(V, width),
            over_q,
            preferred_element_type=F32,
        )

    def swap(p):
        for k in range(OB):
            part = swapped(p, k)
            for l in range(OB):
                acc[k, l] = acc[k, l] - part[l * HALF : (l + 1) * HALF]

    steps = dict(
        j0=j0, i1=i1, j1a=j1a, j1b=j1b, j1c=j1c, j1d=j1d, j2a=j2a, j2b=j2b, i2a=i2a, i2b=i2b,
        j3a=j3a, j3b=j3b, j3c=j3c, j3d=j3d, i3=i3, i4=i4, j4=j4, co0=direct, co1=swap,
    )
    received()
    for name, g in SEQ:
        steps[name](g)

    def send_to(src, dst, kind, i, dev):
        pltpu.make_async_remote_copy(
            src_ref=src, dst_ref=dst, send_sem=gs.at[kind], recv_sem=gr.at[i],
            device_id=dev, device_id_type=MESH,
        ).start()

    def landed(dst, i):
        pltpu.make_async_copy(dst, dst, gr.at[i]).wait()

    plus, minus = pl.ds(0, 128), pl.ds(128, 128)
    rows_of = [pl.ds(k * HALF, HALF) for k in range(OB)]

    def amplitude(k):
        part = swapped(len(PASSES) - 1, k)
        for l in range(OB):
            value = (acc[k, l] - part[l * HALF : (l + 1) * HALF]) * rden[k, l]
            amp[k, :, l * V : (l + 1) * V] = value.astype(BF16)

    def gamma(m, block, ks, r, i):
        total = None
        for l in range(OB):
            value = jnp.dot(
                amp[ks, :, l * V : (l + 1) * V].reshape(-1, V),
                fj[block, l].reshape(V, QC),
                preferred_element_type=F32,
            )
            total = value if total is None else total + value
        low, high = total[:, :HALF], total[:, HALF:]
        sib_s[m, r] = jnp.where(core == 0, high, low).astype(BF16)
        send_to(sib_s.at[m, r], sib_r.at[m, r], 0, i, sib)
        gown[m, r] = jnp.where(core == 0, low, high)

    def near(m, k, block):
        gamma(m, block, slice(k, k + 1), rows_of[k], 3 * m + k)

    def far_send(k):
        r = rows_of[k]
        landed(sib_r.at[0, r], k)
        opp_s[r] = (gown[0, r] + sib_r[0, r].astype(F32)).astype(BF16)
        send_to(opp_s.at[r, plus], opp_r.at[r, plus], 1, 10 + k, xdev(1))
        send_to(opp_s.at[r, minus], opp_r.at[r, minus], 1, 13 + k, xdev(-1))

    def free(m, k):
        r, lanes, dev = rows_of[k], (minus, plus)[m - 1], xdev((1, -1)[m - 1])
        landed(sib_r.at[m, r], 3 * m + k)
        gown[m, r] = gown[m, r] + sib_r[m, r].astype(F32)
        rs_s[m - 1, r, lanes] = gown[m, r, lanes].astype(BF16)
        send_to(rs_s.at[m - 1, r, lanes], rs_r.at[m - 1, r, lanes], 2, 16 + k, dev)

    def relay(m, k):
        r, lanes, dev = rows_of[k], (plus, minus)[m - 1], xdev((1, -1)[m - 1])
        landed(opp_r.at[r, lanes], (10, 13)[m - 1] + k)
        rs_s[m - 1, r, lanes] = (gown[m, r, lanes] + opp_r[r, lanes].astype(F32)).astype(BF16)
        send_to(rs_s.at[m - 1, r, lanes], rs_r.at[m - 1, r, lanes], 2, 16 + k, dev)

    direct(len(PASSES) - 1)
    amplitude(0)
    near(0, 0, x2)
    near(1, 0, xp)
    far_send(0)
    near(2, 0, xm)
    free(1, 0)
    amplitude(1)
    near(0, 1, x2)
    free(2, 0)
    near(1, 1, xp)
    far_send(1)
    relay(1, 0)
    relay(2, 0)
    near(2, 1, xm)
    free(1, 1)
    amplitude(2)
    near(0, 2, x2)
    free(2, 1)
    near(1, 2, xp)
    far_send(2)
    relay(1, 1)
    relay(2, 1)
    near(2, 2, xm)
    free(1, 2)
    gamma(3, x, every, every, 9)
    free(2, 2)
    relay(1, 2)
    relay(2, 2)
    landed(sib_r.at[3], 9)
    gown[3] = gown[3] + sib_r[3].astype(F32)
    results = []
    for k in range(OB):
        r = rows_of[k]
        landed(rs_r.at[:, r], 16 + k)
        total = gown[3, r] + rs_r[0, r].astype(F32) + rs_r[1, r].astype(F32)
        for h in range(2):
            q = pl.ds(h * 128, 128)
            out_ref[k, q] = total[:, h * 128 : (h + 1) * 128].T
            results.append(pltpu.make_async_copy(out_ref.at[k, q], out_hbm.at[k, q], out_sem.at[k, h]))
            results[-1].start()
    def sent(rows, sem):
        size = met.at[0, pl.ds(0, rows)]
        pltpu.make_async_copy(size, size, sem).wait()

    for g in range(NG):
        for kind in range(2):
            sent(45 * (GROUPS[g][2] + GROUPS[g][3]) // 16, ss.at[g, kind])
    for kind, rows in enumerate((2 * ROWS, ROWS // 2, ROWS)):
        sent(rows, gs.at[kind])
    for copy in results:
        copy.wait()
    left = send.at[pl.ds(0, 127)]
    pltpu.make_async_copy(left, left, all_s).wait()


def body(raw_integrals, metric_root, eps_occ, eps_vir):
    pieces = raw_integrals.shape[0]
    aux_total = metric_root.shape[0]
    out = pl.pallas_call(
        kernel,
        out_shape=jax.ShapeDtypeStruct((OB, HALF, HALF), F32),
        in_specs=[pl.BlockSpec(memory_space=pltpu.HBM)] * 4,
        out_specs=pl.BlockSpec(memory_space=pltpu.HBM),
        scratch_shapes=[
            pltpu.VMEM(raw_integrals.shape, BF16),
            pltpu.SMEM(eps_occ.shape, F32),
            pltpu.VMEM((1, V), F32),
            pltpu.VMEM((128, pieces, 128), F32),
            pltpu.VMEM((128, 24, 128), BF16),
            pltpu.VMEM((128, 24, 128), BF16),
            pltpu.VMEM((192, aux_total), BF16),
            pltpu.VMEM((HALF, 128), F32),
            pltpu.VMEM((OB, OB, HALF, V), F32),
            pltpu.VMEM((NC, OB, 4, 2, 2, 32, QC), BF16),
            pltpu.VMEM((NC, OB, 4, 4, 32, QC), BF16),
            pltpu.VMEM((NC, aux_total, QC), BF16),
            pltpu.VMEM((OB, OB, HALF, V), F32),
            pltpu.VMEM((OB, HALF, OB * V), BF16),
            pltpu.VMEM((4, ROWS, HALF), F32),
            pltpu.VMEM((4, ROWS, HALF), BF16),
            pltpu.VMEM((4, ROWS, HALF), BF16),
            pltpu.VMEM((ROWS, HALF), BF16),
            pltpu.VMEM((ROWS, HALF), BF16),
            pltpu.VMEM((2, ROWS, HALF), BF16),
            pltpu.VMEM((2, ROWS, HALF), BF16),
            pltpu.VMEM((OB, HALF, HALF), F32),
            pltpu.SemaphoreType.DMA((NC,)),
            pltpu.SemaphoreType.DMA((3,)),
            pltpu.SemaphoreType.DMA,
            pltpu.SemaphoreType.DMA,
            pltpu.SemaphoreType.DMA((NG, 2)),
            pltpu.SemaphoreType.DMA((NG, 18)),
            pltpu.SemaphoreType.DMA((3,)),
            pltpu.SemaphoreType.DMA((19,)),
            pltpu.SemaphoreType.DMA((OB, 2)),
        ],
        compiler_params=pltpu.CompilerParams(
            collective_id=0, has_side_effects=True, vmem_limit_bytes=60 * 1024 * 1024
        ),
    )(raw_integrals, metric_root, eps_occ, eps_vir.reshape(1, V))
    return out.transpose(1, 0, 2)


def solution(mesh):
    in_specs = (P(("ia", "ja", "aux"), None, None), P(), P(), P())
    out_specs = P("ja", "ia", "aux")
    return jax.shard_map(body, mesh=mesh, in_specs=in_specs, out_specs=out_specs, check_vma=False)
```
